256 devices in a mesh: dp: 8 (over y, x_hi), ctx: 32 (over x_lo, z, core).
Axes of the slice: x: 4 (x_hi: 2, x_lo: 2; x = x_hi * 2 + x_lo), y: 4, z: 8, core: 2. Of those that a mesh axis runs over, the one named last changes fastest.
Arguments:
- inputs: bfloat16 [8, 64, 65536], P('dp', None, 'ctx'), may hold values from -6 to 6
- out_grad: bfloat16 [8, 64, 65536], P('dp', None, 'ctx'), may hold values from -0.0390625 to 0.0390625
- master: float32 [64, 65536], P('ctx', 'dp'), may hold values from -0.0234375 to 0.0234375
- moment_one: float32 [64, 65536], P('ctx', 'dp'), may hold values from -6 to 6
- moment_two: float32 [64, 65536], P('ctx', 'dp'), may hold values from 0.05 to 1
- next_inputs: bfloat16 [8, 64, 65536], P('dp', None, 'ctx'), may hold values from -6 to 6
Outputs:
- new_master: float32 [64, 65536], P('ctx', 'dp')
- new_moment_one: float32 [64, 65536], P('ctx', 'dp')
- new_moment_two: float32 [64, 65536], P('ctx', 'dp')
- next_out: bfloat16 [8, 64, 65536], P('dp', None, 'ctx')
The draws below stay inside these ranges and needn't reach their ends.
All inputs are finite; a program needn't handle non-finite values.
Results may differ from the reference program's by a relative error of at most 0.007.
Values may be sent and summed in bfloat16 or wider, within the bound.
No kernel may reach another device: no remote copies, remote signals or barrier semaphores. Data moves between devices by JAX's collectives and lax.ppermute only.
A program may use at most 128 MiB of HBM per device.

```python
import math
import jax
import jax.numpy as jnp
from jax import lax

TAPS = 65536
CH = 64
DP = 8


def steps_of(rng, dims, pieces, least, largest):
    def one(dim, shards_of):
        steps = jax.random.uniform(jax.random.fold_in(jax.random.fold_in(rng, 6), dim), (shards_of,), jnp.float32, least / len(pieces), largest / len(pieces))
        return jnp.repeat(jnp.exp(steps), dims[dim] // shards_of).reshape((-1,) + (1,) * (len(dims) - dim - 1))

    factor_of = one(*pieces[0])
    for cut in pieces[1:]:
        factor_of = factor_of * one(*cut)
    return factor_of


def centred(stream_key, shape, deviation, reach, cuts=(), held_as=jnp.bfloat16):
    loudness = steps_of(stream_key, shape, cuts, -0.22, 0.18) if cuts else 1.0
    values = jax.random.normal(stream_key, shape, jnp.float32) * deviation * loudness
    return jnp.minimum(jnp.maximum(values, -reach), reach).astype(held_as)


def setup_inputs(seed: int = 0) -> dict:
    key_list = jax.random.split(jax.random.key(seed), 7)
    inputs = centred(key_list[0], (DP, CH, TAPS), 1.0, 6.0, ((0, 8), (2, 32)))
    out_grad = centred(key_list[1], (DP, CH, TAPS), (2.0 * (DP * TAPS) ** -0.5), 0.0390625, ((0, 8), (2, 32)))
    master = centred(key_list[2], (CH, TAPS), TAPS ** -0.5, 0.0234375, ((0, 32), (1, 8)), jnp.float32)
    moment_one = centred(key_list[3], (CH, TAPS), 0.5, 6.0, ((0, 32), (1, 8)), jnp.float32)
    moment_two = jnp.clip(jnp.exp(math.log(1.0) - 2.9957323 * jax.random.uniform(key_list[4], (CH, TAPS), jnp.float32) ** steps_of(key_list[4], (CH, TAPS), ((0, 32), (1, 8)), -0.2, 0.2)), 0.05, 1.0)
    next_inputs = centred(key_list[5], (DP, CH, TAPS), 1.0, 6.0, ((0, 8), (2, 32)))
    return dict(inputs=inputs, out_grad=out_grad, master=master, moment_one=moment_one, moment_two=moment_two, next_inputs=next_inputs)


def reference(inputs, out_grad, master, moment_one, moment_two, next_inputs):
    length = 2 * TAPS
    seq_spec = jnp.fft.rfft(inputs.astype(jnp.float32), n=length, axis=-1)
    grad_spec = jnp.fft.rfft(out_grad.astype(jnp.float32), n=length, axis=-1)
    corr = jnp.fft.irfft(jnp.conj(seq_spec) * grad_spec, n=length, axis=-1)[..., :TAPS]
    grad = lax.optimization_barrier(jnp.sum(corr, axis=0))
    new_one = 0.9 * moment_one + 0.1 * grad
    new_two = 0.999 * moment_two + 0.001 * grad * grad
    first_hat = new_one / (1.0 - 0.9 ** 10)
    second_hat = new_two / (1.0 - 0.999 ** 10)
    new_master = master - 0.01 * (first_hat / (jnp.sqrt(second_hat) + 1e-08) + 0.1 * master)
    filters = new_master.astype(jnp.bfloat16).astype(jnp.float32)
    filter_spec = jnp.fft.rfft(filters, n=length, axis=-1)
    next_spec = jnp.fft.rfft(next_inputs.astype(jnp.float32), n=length, axis=-1)
    result = jnp.fft.irfft(next_spec * filter_spec[None], n=length, axis=-1)[..., :TAPS]
    return (new_master, new_one, new_two, result.astype(jnp.bfloat16))
```

```python
import math

import jax
import jax.numpy as jnp
import numpy as np
from jax import lax
from jax.experimental import pallas as pl
from jax.experimental.pallas import tpu as pltpu
from jax.sharding import PartitionSpec as P

ROWS = 512
LANES = 128
BLOCK = 128

f32 = jnp.float32
bf16 = jnp.bfloat16


def split_table(values):
    high = values.astype(bf16)
    low = (values - high.astype(np.float64)).astype(bf16)
    return high, low


def tables():
    half = np.arange(ROWS) + 0.5
    lanes = np.arange(LANES)
    outer = 2.0 * math.pi * np.outer(half, half) / (2 * ROWS)
    long_side = np.concatenate([np.cos(outer), np.sin(outer)], axis=1)
    turn = 2.0 * math.pi * np.outer(half, lanes / (2.0 * ROWS * LANES) - 1.0 / (4 * ROWS))
    twiddle = np.concatenate([np.cos(turn), np.sin(turn)], axis=1).astype(np.float32)
    inner = 2.0 * math.pi * (np.outer(lanes, lanes) % LANES) / LANES
    cosine, sine = np.cos(inner), np.sin(inner)
    short = np.block([[cosine, sine], [-sine, cosine]])
    short_hi, short_lo = split_table(short)
    long_hi, long_lo = split_table(long_side)
    return (long_hi, long_lo, twiddle, short_hi, short_lo, short_hi.T.copy(), short_lo.T.copy())


def dot(left, right):
    return jnp.dot(left, right, preferred_element_type=f32)


def halves(values):
    high = values.astype(bf16)
    return high, (values - high.astype(f32)).astype(bf16)


def times_short(values, hi_ref, lo_ref):
    high, low = halves(values)
    rows = values.shape[0]
    both = dot(jnp.concatenate([high, low], axis=0), hi_ref[...])
    return both[:rows] + both[rows:] + dot(high, lo_ref[...])


def forward_block(start, waves, long_hi, long_lo, twiddle, short_hi, short_lo):
    rows = pl.ds(start, BLOCK)
    left = jnp.concatenate(
        [long_hi[rows, :ROWS], long_hi[rows, ROWS:], long_lo[rows, :ROWS], long_lo[rows, ROWS:]], axis=0
    )
    cosine, sine = twiddle[rows, :LANES], twiddle[rows, LANES:]
    turned = []
    for wave in waves:
        first = dot(left, wave)
        first = first[: 2 * BLOCK] + first[2 * BLOCK :]
        for c in range(wave.shape[1] // LANES):
            real = first[:BLOCK, c * LANES : (c + 1) * LANES]
            imag = first[BLOCK:, c * LANES : (c + 1) * LANES]
            turned.append(
                jnp.concatenate([real * cosine - imag * sine, real * sine + imag * cosine], axis=1)
            )
    spectra = times_short(jnp.concatenate(turned, axis=0), short_hi, short_lo)
    return [spectra[i * BLOCK : (i + 1) * BLOCK] for i in range(len(turned))]


def backward_block(start, products, twiddle, back_hi, back_lo, high_ref, low_ref):
    rows = pl.ds(start, BLOCK)
    cosine, sine = twiddle[rows, :LANES], twiddle[rows, LANES:]
    mixed = times_short(jnp.concatenate(products, axis=0), back_hi, back_lo)
    for c in range(len(products)):
        real = mixed[c * BLOCK : (c + 1) * BLOCK, :LANES]
        imag = mixed[c * BLOCK : (c + 1) * BLOCK, LANES:]
        lanes = slice(c * LANES, (c + 1) * LANES)
        for at, part in ((start, real * cosine + imag * sine), (ROWS + start, imag * cosine - real * sine)):
            high, low = halves(part)
            high_ref[pl.ds(at, BLOCK), lanes] = high
            low_ref[pl.ds(at, BLOCK), lanes] = low


def last_stage(long_hi, long_lo, high_ref, low_ref):
    left = jnp.concatenate([long_hi[...], long_lo[...]], axis=0)
    both = dot(left, high_ref[...])
    total = both[:ROWS] + both[ROWS:] + dot(long_hi[...], low_ref[...])
    return total * (1.0 / (ROWS * LANES))


def wave_of(ref, first):
    parts = [ref[:, first + c].reshape(ROWS, LANES) for c in range(2)]
    return jnp.concatenate(parts, axis=1)


def pack_body(*refs):
    count = len(refs) // 2 - 1 + len(refs) % 2
    sources, out_ref, scratch = refs[:count], refs[count], refs[count + 1 :]
    for i, ref in enumerate(sources):
        values = ref[...].astype(f32)
        channels, length = values.shape
        pieces = length // LANES
        for k in range(pieces):
            scratch[i][pl.ds(k, channels, stride=pieces), :] = values[:, k * LANES : (k + 1) * LANES]
        peers = out_ref.shape[0]
        out_ref[:, 2 * i : 2 * i + 2] = scratch[i][...].reshape(peers, 2, pieces, LANES).astype(bf16)


def unpack_body(in_ref, out_ref, scratch):
    channels, length = out_ref.shape
    pieces = length // LANES
    scratch[...] = in_ref[...].astype(f32).reshape(channels * pieces, LANES)
    for k in range(pieces):
        out_ref[:, k * LANES : (k + 1) * LANES] = scratch[pl.ds(k, channels, stride=pieces), :].astype(bf16)


def correlate_body(
    in_ref, long_hi, long_lo, twiddle, short_hi, short_lo, back_hi, back_lo, out_ref, high_ref, low_ref, scratch
):
    seq, grad = wave_of(in_ref, 0), wave_of(in_ref, 2)

    def step(b, carry):
        start = pl.multiple_of(b * BLOCK, BLOCK)
        spectra = forward_block(start, (seq, grad), long_hi, long_lo, twiddle, short_hi, short_lo)
        products = []
        for c in range(2):
            s_re, s_im = spectra[c][:, :LANES], spectra[c][:, LANES:]
            g_re, g_im = spectra[2 + c][:, :LANES], spectra[2 + c][:, LANES:]
            products.append(
                jnp.concatenate([g_re * s_re + g_im * s_im, g_im * s_re - g_re * s_im], axis=1)
            )
        backward_block(start, products, twiddle, back_hi, back_lo, high_ref, low_ref)
        return carry

    lax.fori_loop(0, ROWS // BLOCK, step, 0)
    result = last_stage(long_hi, long_lo, high_ref, low_ref)
    for c in range(2):
        scratch[pl.ds(c, ROWS, stride=2), :] = result[:, c * LANES : (c + 1) * LANES]
    out_ref[...] = scratch[...].astype(bf16).reshape(out_ref.shape)


def adam_body(grad_ref, master, one, two, new_master, new_one, new_two, filters):
    grad = grad_ref[0].astype(f32)
    for q in range(1, grad_ref.shape[0]):
        grad = grad + grad_ref[q].astype(f32)
    first = 0.9 * one[...] + 0.1 * grad
    second = 0.999 * two[...] + 0.001 * grad * grad
    new_one[...] = first
    new_two[...] = second
    first_hat = first / (1.0 - 0.9**10)
    second_hat = second / (1.0 - 0.999**10)
    old = master[...]
    new = old - 0.01 * (first_hat / (jnp.sqrt(second_hat) + 1e-08) + 0.1 * old)
    new_master[...] = new
    rounded = new.astype(bf16)
    for q in range(filters.shape[0]):
        filters[q] = rounded


def spectrum_body(in_ref, long_hi, long_lo, twiddle, short_hi, short_lo, out_ref):
    wave = wave_of(in_ref, 0)

    def step(b, carry):
        start = pl.multiple_of(b * BLOCK, BLOCK)
        spectra = forward_block(start, (wave,), long_hi, long_lo, twiddle, short_hi, short_lo)
        for c in range(2):
            out_ref[c, pl.ds(start, BLOCK), :] = spectra[c]
        return carry

    lax.fori_loop(0, ROWS // BLOCK, step, 0)


def convolve_body(
    in_ref, next_ref, long_hi, long_lo, twiddle, short_hi, short_lo, back_hi, back_lo,
    out_ref, high_ref, low_ref, scratch,
):
    scratch[...] = in_ref[...].reshape(2 * ROWS, LANES).astype(f32)
    wave = jnp.concatenate(
        [scratch[pl.ds(c, ROWS, stride=2), :].astype(bf16) for c in range(2)], axis=1
    )

    def step(b, carry):
        start = pl.multiple_of(b * BLOCK, BLOCK)
        spectra = forward_block(start, (wave,), long_hi, long_lo, twiddle, short_hi, short_lo)
        products = []
        for c in range(2):
            f_re, f_im = spectra[c][:, :LANES], spectra[c][:, LANES:]
            n_re = next_ref[c, pl.ds(start, BLOCK), :LANES]
            n_im = next_ref[c, pl.ds(start, BLOCK), LANES:]
            products.append(
                jnp.concatenate([f_re * n_re - f_im * n_im, f_re * n_im + f_im * n_re], axis=1)
            )
        backward_block(start, products, twiddle, back_hi, back_lo, high_ref, low_ref)
        return carry

    lax.fori_loop(0, ROWS // BLOCK, step, 0)
    result = last_stage(long_hi, long_lo, high_ref, low_ref).astype(bf16)
    peers, pieces = out_ref.shape[0], out_ref.shape[2]
    for c in range(2):
        out_ref[:, c] = result[:, c * LANES : (c + 1) * LANES].reshape(peers, pieces, LANES)


def call(body, name, out_shape, scratch, *args):
    return pl.pallas_call(
        body,
        out_shape=out_shape,
        in_specs=[pl.BlockSpec(memory_space=pltpu.VMEM)] * len(args),
        out_specs=jax.tree.map(lambda _: pl.BlockSpec(memory_space=pltpu.VMEM), out_shape),
        scratch_shapes=scratch,
        name=name,
    )(*args)


def shape(dims, dtype):
    return jax.ShapeDtypeStruct(dims, dtype)


def interleave(values):
    channels, taps = values.shape
    pieces = taps // LANES
    return values.reshape(channels, pieces, LANES).transpose(1, 0, 2).reshape(channels * pieces, LANES)


def deinterleave(values, channels):
    pieces = values.shape[0] // channels
    return values.reshape(pieces, channels, LANES).transpose(1, 0, 2).reshape(channels, pieces * LANES)


def exchange(values, axis):
    return lax.all_to_all(values, axis, split_axis=0, concat_axis=0, tiled=True)


def local(inputs, out_grad, master, moment_one, moment_two, next_inputs):
    channels, length = inputs.shape[1:]
    peers = lax.axis_size("ctx")
    owners = lax.axis_size("dp")
    pieces = length // LANES
    rows = channels * pieces
    long_hi, long_lo, twiddle, short_hi, short_lo, back_hi, back_lo = (jnp.asarray(t) for t in tables())
    ahead = (long_hi, long_lo, twiddle, short_hi, short_lo)
    work = [pltpu.VMEM((2 * ROWS, 2 * LANES), bf16)] * 2 + [pltpu.VMEM((2 * ROWS, LANES), f32)]

    packed = call(
        pack_body, "pack", shape((peers, 4, pieces, LANES), bf16), [pltpu.VMEM((rows, LANES), f32)] * 2,
        inputs[0], out_grad[0],
    )
    next_packed = call(
        pack_body, "pack_next", shape((peers, 2, pieces, LANES), bf16), [pltpu.VMEM((rows, LANES), f32)],
        next_inputs[0],
    )
    partial = call(
        correlate_body, "correlate", shape((owners, 2 * ROWS // owners, LANES), bf16), work,
        exchange(packed, "ctx"), *ahead, back_hi, back_lo,
    )
    partials = exchange(partial, "dp")
    own = shape((2 * ROWS // owners, LANES), f32)
    new_master, new_one, new_two, filters = call(
        adam_body, "adam", (own, own, own, shape(partial.shape, bf16)), [],
        partials, interleave(master), interleave(moment_one), interleave(moment_two),
    )
    next_spectrum = call(
        spectrum_body, "spectrum", shape((2, ROWS, 2 * LANES), f32), [], exchange(next_packed, "ctx"), *ahead
    )
    result = call(
        convolve_body, "convolve", shape((peers, 2, pieces, LANES), bf16), work,
        exchange(filters, "dp"), next_spectrum, *ahead, back_hi, back_lo,
    )
    next_out = call(
        unpack_body, "unpack", shape((channels, length), bf16), [pltpu.VMEM((rows, LANES), f32)],
        exchange(result, "ctx"),
    )
    return (deinterleave(new_master, 2), deinterleave(new_one, 2), deinterleave(new_two, 2), next_out[None])


def solution(mesh):
    return jax.shard_map(
        local,
        mesh=mesh,
        in_specs=(
            P("dp", None, "ctx"),
            P("dp", None, "ctx"),
            P("ctx", "dp"),
            P("ctx", "dp"),
            P("ctx", "dp"),
            P("dp", None, "ctx"),
        ),
        out_specs=(P("ctx", "dp"), P("ctx", "dp"), P("ctx", "dp"), P("dp", None, "ctx")),
        check_vma=False,
    )
```

```python
import math

import jax
import jax.numpy as jnp
import numpy as np
from jax import lax
from jax.experimental import pallas as pl
from jax.experimental.pallas import tpu as pltpu
from jax.sharding import PartitionSpec as P

ROWS = 512
LANES = 128
BLOCK = 128

f32 = jnp.float32
bf16 = jnp.bfloat16


def split_table(values):
    high = values.astype(bf16)
    low = (values - high.astype(np.float64)).astype(bf16)
    return high, low


def tables():
    half = np.arange(ROWS) + 0.5
    lanes = np.arange(LANES)
    outer = 2.0 * math.pi * np.outer(half, half) / (2 * ROWS)
    long_side = np.concatenate([np.cos(outer), np.sin(outer)], axis=1)
    turn = 2.0 * math.pi * np.outer(half, lanes / (2.0 * ROWS * LANES) - 1.0 / (4 * ROWS))
    twiddle = np.concatenate([np.cos(turn), np.sin(turn)], axis=1).astype(np.float32)
    inner = 2.0 * math.pi * (np.outer(lanes, lanes) % LANES) / LANES
    cosine, sine = np.cos(inner), np.sin(inner)
    short = np.block([[cosine, sine], [-sine, cosine]])
    short_hi, short_lo = split_table(short)
    long_hi, long_lo = split_table(long_side)
    return (long_hi, long_lo, twiddle, short_hi, short_lo, short_hi.T.copy(), short_lo.T.copy())


def dot(left, right):
    return jnp.dot(left, right, preferred_element_type=f32)


def halves(values):
    high = values.astype(bf16)
    return high, (values - high.astype(f32)).astype(bf16)


def times_short(values, hi_ref, lo_ref):
    high, low = halves(values)
    rows = values.shape[0]
    both = dot(jnp.concatenate([high, low], axis=0), hi_ref[...])
    return both[:rows] + both[rows:] + dot(high, lo_ref[...])


def forward_block(start, waves, long_hi, long_lo, twiddle, short_hi, short_lo):
    rows = pl.ds(start, BLOCK)
    left = jnp.concatenate(
        [long_hi[rows, :ROWS], long_hi[rows, ROWS:], long_lo[rows, :ROWS], long_lo[rows, ROWS:]], axis=0
    )
    cosine, sine = twiddle[rows, :LANES], twiddle[rows, LANES:]
    turned = []
    for wave in waves:
        first = dot(left, wave)
        first = first[: 2 * BLOCK] + first[2 * BLOCK :]
        for c in range(wave.shape[1] // LANES):
            real = first[:BLOCK, c * LANES : (c + 1) * LANES]
            imag = first[BLOCK:, c * LANES : (c + 1) * LANES]
            turned.append(
                jnp.concatenate([real * cosine - imag * sine, real * sine + imag * cosine], axis=1)
            )
    spectra = times_short(jnp.concatenate(turned, axis=0), short_hi, short_lo)
    return [spectra[i * BLOCK : (i + 1) * BLOCK] for i in range(len(turned))]


def backward_block(start, products, twiddle, back_hi, back_lo, high_ref, low_ref):
    rows = pl.ds(start, BLOCK)
    cosine, sine = twiddle[rows, :LANES], twiddle[rows, LANES:]
    mixed = times_short(jnp.concatenate(products, axis=0), back_hi, back_lo)
    for c in range(len(products)):
        real = mixed[c * BLOCK : (c + 1) * BLOCK, :LANES]
        imag = mixed[c * BLOCK : (c + 1) * BLOCK, LANES:]
        lanes = slice(c * LANES, (c + 1) * LANES)
        for at, part in ((start, real * cosine + imag * sine), (ROWS + start, imag * cosine - real * sine)):
            high, low = halves(part)
            high_ref[pl.ds(at, BLOCK), lanes] = high
            low_ref[pl.ds(at, BLOCK), lanes] = low


def last_stage(long_hi, long_lo, high_ref, low_ref):
    left = jnp.concatenate([long_hi[...], long_lo[...]], axis=0)
    both = dot(left, high_ref[...])
    total = both[:ROWS] + both[ROWS:] + dot(long_hi[...], low_ref[...])
    return total * (1.0 / (ROWS * LANES))


def wave_of(ref, first):
    parts = [ref[:, first + c].reshape(ROWS, LANES) for c in range(2)]
    return jnp.concatenate(parts, axis=1)


def fetch(sources, places, semaphores):
    copies = [
        pltpu.make_async_copy(source, place, semaphores.at[i])
        for i, (source, place) in enumerate(zip(sources, places))
    ]
    for copy in copies:
        copy.start()
    return copies


def pack_body(*refs):
    count = (len(refs) - 2) // 3
    sources, out_ref, semaphores = refs[:count], refs[count], refs[-1]
    arrived, scratch = refs[count + 1 : 2 * count + 1], refs[2 * count + 1 : -1]
    copies = fetch(sources, arrived, semaphores)
    peers, _, pieces, _ = out_ref.shape
    for i in range(count):
        copies[i].wait()
        channels = arrived[i].shape[0]
        for k in range(pieces):
            lanes = slice(k * LANES, (k + 1) * LANES)
            scratch[i][pl.ds(k, channels, stride=pieces), :] = arrived[i][:, lanes].astype(f32)
        out_ref[:, 2 * i : 2 * i + 2] = scratch[i][...].reshape(peers, 2, pieces, LANES).astype(bf16)


def unpack_body(in_ref, out_ref, scratch):
    channels, length = out_ref.shape
    pieces = length // LANES
    scratch[...] = in_ref[...].astype(f32).reshape(channels * pieces, LANES)
    for k in range(pieces):
        out_ref[:, k * LANES : (k + 1) * LANES] = scratch[pl.ds(k, channels, stride=pieces), :].astype(bf16)


def correlate_body(
    in_ref, long_hi, long_lo, twiddle, short_hi, short_lo, back_hi, back_lo, out_ref, high_ref, low_ref, scratch
):
    seq, grad = wave_of(in_ref, 0), wave_of(in_ref, 2)

    def step(b, carry):
        start = pl.multiple_of(b * BLOCK, BLOCK)
        spectra = forward_block(start, (seq, grad), long_hi, long_lo, twiddle, short_hi, short_lo)
        products = []
        for c in range(2):
            s_re, s_im = spectra[c][:, :LANES], spectra[c][:, LANES:]
            g_re, g_im = spectra[2 + c][:, :LANES], spectra[2 + c][:, LANES:]
            products.append(
                jnp.concatenate([g_re * s_re + g_im * s_im, g_im * s_re - g_re * s_im], axis=1)
            )
        backward_block(start, products, twiddle, back_hi, back_lo, high_ref, low_ref)
        return carry

    lax.fori_loop(0, ROWS // BLOCK, step, 0)
    result = last_stage(long_hi, long_lo, high_ref, low_ref)
    for c in range(2):
        scratch[pl.ds(c, ROWS, stride=2), :] = result[:, c * LANES : (c + 1) * LANES]
    out_ref[...] = scratch[...].astype(bf16).reshape(out_ref.shape)


def adam_body(grad_ref, master, one, two, new_master, new_one, new_two, filters, rounded, semaphores):
    grad = grad_ref[0].astype(f32)
    for q in range(1, grad_ref.shape[0]):
        grad = grad + grad_ref[q].astype(f32)
    first = 0.9 * one[...] + 0.1 * grad
    second = 0.999 * two[...] + 0.001 * grad * grad
    first_hat = first / (1.0 - 0.9**10)
    second_hat = second / (1.0 - 0.999**10)
    old = master[...]
    new = old - 0.01 * (first_hat / (jnp.sqrt(second_hat) + 1e-08) + 0.1 * old)
    rounded[...] = new.astype(bf16)
    owners = filters.shape[0]
    copies = fetch([rounded] * owners, [filters.at[q] for q in range(owners)], semaphores)
    new_one[...] = first
    new_two[...] = second
    new_master[...] = new
    for copy in copies:
        copy.wait()


def spectrum_body(in_ref, long_hi, long_lo, twiddle, short_hi, short_lo, out_ref, result, semaphores):
    wave = wave_of(in_ref, 4)
    copies = []
    for b in range(ROWS // BLOCK):
        start = b * BLOCK
        rows = pl.ds(start, BLOCK)
        spectra = forward_block(start, (wave,), long_hi, long_lo, twiddle, short_hi, short_lo)
        for c in range(2):
            result[c, rows, :] = spectra[c]
        copies += fetch([result.at[:, rows, :]], [out_ref.at[:, rows, :]], semaphores.at[pl.ds(b, 1)])
    for copy in copies:
        copy.wait()


def convolve_body(
    long_hi, long_lo, in_hbm, next_hbm, twiddle_hbm, short_hi_hbm, short_lo_hbm, back_hi_hbm, back_lo_hbm,
    out_ref, high_ref, low_ref, scratch, in_ref, next_ref, twiddle, short_hi, short_lo, back_hi, back_lo, semaphores,
):
    copies = fetch(
        (in_hbm, twiddle_hbm, short_hi_hbm, short_lo_hbm, next_hbm, back_hi_hbm, back_lo_hbm),
        (in_ref, twiddle, short_hi, short_lo, next_ref, back_hi, back_lo),
        semaphores,
    )
    copies[0].wait()
    scratch[...] = in_ref[...].reshape(2 * ROWS, LANES).astype(f32)
    wave = jnp.concatenate(
        [scratch[pl.ds(c, ROWS, stride=2), :].astype(bf16) for c in range(2)], axis=1
    )
    for copy in copies[1:]:
        copy.wait()

    def step(b, carry):
        start = pl.multiple_of(b * BLOCK, BLOCK)
        spectra = forward_block(start, (wave,), long_hi, long_lo, twiddle, short_hi, short_lo)
        products = []
        for c in range(2):
            f_re, f_im = spectra[c][:, :LANES], spectra[c][:, LANES:]
            n_re = next_ref[c, pl.ds(start, BLOCK), :LANES]
            n_im = next_ref[c, pl.ds(start, BLOCK), LANES:]
            products.append(
                jnp.concatenate([f_re * n_re - f_im * n_im, f_re * n_im + f_im * n_re], axis=1)
            )
        backward_block(start, products, twiddle, back_hi, back_lo, high_ref, low_ref)
        return carry

    lax.fori_loop(0, ROWS // BLOCK, step, 0)
    result = last_stage(long_hi, long_lo, high_ref, low_ref).astype(bf16)
    peers, pieces = out_ref.shape[0], out_ref.shape[2]
    for c in range(2):
        out_ref[:, c] = result[:, c * LANES : (c + 1) * LANES].reshape(peers, pieces, LANES)


def call(body, name, out_shape, scratch, *args, far=(), far_out=False):
    near = [pltpu.with_memory_space_constraint(a, pltpu.VMEM) for a in args]
    far = [pltpu.with_memory_space_constraint(a, pltpu.HBM) for a in far]
    inside, outside = pl.BlockSpec(memory_space=pltpu.VMEM), pl.BlockSpec(memory_space=pltpu.HBM)
    out_specs = [inside] * len(out_shape)
    if far_out:
        out_specs[-1] = outside
        out_shape = (*out_shape[:-1], pltpu.HBM(out_shape[-1].shape, out_shape[-1].dtype))
    return pl.pallas_call(
        body,
        out_shape=out_shape,
        in_specs=[inside] * len(near) + [outside] * len(far),
        out_specs=tuple(out_specs),
        scratch_shapes=scratch,
        name=name,
        compiler_params=pltpu.CompilerParams(vmem_limit_bytes=16 << 20),
    )(*near, *far)


def shape(dims, dtype):
    return jax.ShapeDtypeStruct(dims, dtype)


def interleave(values):
    channels, taps = values.shape
    pieces = taps // LANES
    return values.reshape(channels, pieces, LANES).transpose(1, 0, 2).reshape(channels * pieces, LANES)


def deinterleave(values, channels):
    pieces = values.shape[0] // channels
    return values.reshape(pieces, channels, LANES).transpose(1, 0, 2).reshape(channels, pieces * LANES)


def exchange(values, axis):
    return lax.all_to_all(values, axis, split_axis=0, concat_axis=0, tiled=True)


def local(inputs, out_grad, master, moment_one, moment_two, next_inputs):
    channels, length = inputs.shape[1:]
    peers = lax.axis_size("ctx")
    owners = lax.axis_size("dp")
    pieces = length // LANES
    rows = channels * pieces
    long_hi, long_lo, twiddle, short_hi, short_lo, back_hi, back_lo = (jnp.asarray(t) for t in tables())
    ahead = (long_hi, long_lo, twiddle, short_hi, short_lo)
    work = [pltpu.VMEM((2 * ROWS, 2 * LANES), bf16)] * 2 + [pltpu.VMEM((2 * ROWS, LANES), f32)]

    sources = (inputs[0], out_grad[0], next_inputs[0])
    (packed,) = call(
        pack_body, "pack", (shape((peers, 6, pieces, LANES), bf16),),
        [pltpu.VMEM((channels, length), bf16)] * 3 + [pltpu.VMEM((rows, LANES), f32)] * 3
        + [pltpu.SemaphoreType.DMA((3,))],
        far=sources,
    )
    waves = exchange(packed, "ctx")
    own = (2 * ROWS // owners, LANES)
    (partial,) = call(
        correlate_body, "correlate", (shape((owners, *own), bf16),), work, waves, *ahead, back_hi, back_lo
    )
    new_master, new_one, new_two, filters = call(
        adam_body, "adam", (shape(own, f32),) * 3 + (shape((owners, *own), bf16),),
        [pltpu.VMEM(own, bf16), pltpu.SemaphoreType.DMA((owners,))],
        exchange(partial, "dp"), interleave(master), interleave(moment_one), interleave(moment_two), far_out=True,
    )
    spectra = (2, ROWS, 2 * LANES)
    (next_spectrum,) = call(
        spectrum_body, "spectrum", (shape(spectra, f32),),
        [pltpu.VMEM(spectra, f32), pltpu.SemaphoreType.DMA((ROWS // BLOCK,))], waves, *ahead, far_out=True,
    )
    far = (exchange(filters, "dp"), next_spectrum, twiddle, short_hi, short_lo, back_hi, back_lo)
    (result,) = call(
        convolve_body, "convolve", (shape((peers, 2, pieces, LANES), bf16),),
        work + [pltpu.VMEM(t.shape, t.dtype) for t in far] + [pltpu.SemaphoreType.DMA((len(far),))],
        long_hi, long_lo, far=far,
    )
    (next_out,) = call(
        unpack_body, "unpack", (shape((channels, length), bf16),), [pltpu.VMEM((rows, LANES), f32)],
        exchange(result, "ctx"),
    )
    return (deinterleave(new_master, 2), deinterleave(new_one, 2), deinterleave(new_two, 2), next_out[None])


def solution(mesh):
    return jax.shard_map(
        local,
        mesh=mesh,
        in_specs=(
            P("dp", None, "ctx"),
            P("dp", None, "ctx"),
            P("ctx", "dp"),
            P("ctx", "dp"),
            P("ctx", "dp"),
            P("dp", None, "ctx"),
        ),
        out_specs=(P("ctx", "dp"), P("ctx", "dp"), P("ctx", "dp"), P("dp", None, "ctx")),
        check_vma=False,
    )
```

```python
import math

import jax
import jax.numpy as jnp
import numpy as np
from jax import lax
from jax.experimental import pallas as pl
from jax.experimental.pallas import tpu as pltpu
from jax.sharding import PartitionSpec as P

ROWS = 512
LANES = 128
BLOCK = 128

f32 = jnp.float32
bf16 = jnp.bfloat16


def split_table(values):
    high = values.astype(bf16)
    low = (values - high.astype(np.float64)).astype(bf16)
    return high, low


def tables():
    half = np.arange(ROWS) + 0.5
    lanes = np.arange(LANES)
    outer = 2.0 * math.pi * np.outer(half, half) / (2 * ROWS)
    long_hi, long_lo = split_table(np.concatenate([np.cos(outer), np.sin(outer)], axis=0))
    turn = 2.0 * math.pi * np.outer(half, lanes / (2.0 * ROWS * LANES) - 1.0 / (4 * ROWS))
    twiddle = np.concatenate([np.cos(turn), np.sin(turn)], axis=1).astype(np.float32)
    inner = 2.0 * math.pi * (np.outer(lanes, lanes) % LANES) / LANES
    cosine, sine = np.cos(inner), np.sin(inner)
    short = np.block([[cosine, sine], [-sine, cosine]])
    short_hi, short_lo = split_table(short)
    fore, rear = slice(0, ROWS // 2), slice(ROWS // 2, ROWS)
    double = lambda part: (2.0 * part.astype(np.float64)).astype(bf16)
    long = np.concatenate(
        [long_hi[:, fore], long_lo[:, fore], double(long_hi[:, rear]), double(long_lo[:, rear])], axis=1
    )
    return (long, twiddle, short_hi, short_lo)


def dot(left, right):
    return jnp.dot(left, right, preferred_element_type=f32)


def store_halves(values, place, high_ref, low_ref):
    high = values.astype(bf16)
    high_ref[place] = high
    low_ref[place] = (values - high.astype(f32)).astype(bf16)


def times_short(high_ref, low_ref, rows, hi_ref, lo_ref):
    left = jnp.concatenate([high_ref[rows], low_ref[rows], high_ref[rows]], axis=1)
    right = jnp.concatenate([hi_ref[...], hi_ref[...], lo_ref[...]], axis=0)
    return dot(left, right)


def channel_rows(c):
    return slice(c * ROWS, (c + 1) * ROWS)


def channel_lanes(c):
    return slice(c * LANES, (c + 1) * LANES)


def forward(waves, long, twiddle, short_hi, short_lo, high_ref, low_ref):
    left, right = slice(0, LANES), slice(LANES, 2 * LANES)
    half = ROWS // 2
    spectra = []
    for wave in waves:
        fore = dot(long[:, :ROWS], jnp.concatenate([wave[:half], wave[:half]], axis=0))
        rear = dot(long[:, ROWS:], jnp.concatenate([wave[half:], wave[half:]], axis=0))
        first = fore + 0.5 * rear
        done = len(spectra)
        for c in range(2):
            at = channel_rows(done + c)
            real, imag = first[:ROWS, channel_lanes(c)], first[ROWS:, channel_lanes(c)]
            cosine, sine = twiddle[:, left], twiddle[:, right]
            store_halves(real * cosine - imag * sine, (at, left), high_ref, low_ref)
            store_halves(real * sine + imag * cosine, (at, right), high_ref, low_ref)
        for c in range(2):
            spectra.append(times_short(high_ref, low_ref, channel_rows(done + c), short_hi, short_lo))
    return spectra


def backward(products, long, twiddle, short_hi, short_lo, high_ref, low_ref, wide_hi, wide_lo):
    left, right = slice(0, LANES), slice(LANES, 2 * LANES)
    half = ROWS // 2
    top, end = slice(0, ROWS), slice(ROWS, 2 * ROWS)
    for c, (real, imag) in enumerate(products):
        store_halves(real, (channel_rows(c), left), high_ref, low_ref)
        store_halves(-imag, (channel_rows(c), right), high_ref, low_ref)
    mixed = [
        times_short(high_ref, low_ref, channel_rows(c), short_hi, short_lo) for c in range(len(products))
    ]
    for c in range(len(products)):
        cosine, sine = twiddle[:, left], twiddle[:, right]
        mixed_re, mixed_im = mixed[c][:, left], mixed[c][:, right]
        store_halves(mixed_re * cosine - mixed_im * sine, (top, channel_lanes(c)), wide_hi, wide_lo)
        store_halves(-(mixed_im * cosine + mixed_re * sine), (end, channel_lanes(c)), wide_hi, wide_lo)
    total = []
    for at in (0, half):
        both, high = slice(2 * at, 2 * at + ROWS), slice(2 * at, 2 * at + half)
        real, imag = slice(at, at + half), slice(ROWS + at, ROWS + at + half)
        table = jnp.concatenate([long[top, both], long[end, both], long[top, high], long[end, high]], axis=1)
        waves = [wide_hi[real], wide_hi[real], wide_hi[imag], wide_hi[imag], wide_lo[real], wide_lo[imag]]
        total.append(dot(table, jnp.concatenate(waves, axis=0)))
    scale = 1.0 / (ROWS * LANES)
    return total[0] * scale + total[1] * (0.5 * scale)


def wave_of(ref, first):
    parts = [ref[:, first + c].reshape(ROWS, LANES) for c in range(2)]
    return jnp.concatenate(parts, axis=1)


def fetch(sources, places, semaphores):
    copies = [
        pltpu.make_async_copy(source, place, semaphores.at[i])
        for i, (source, place) in enumerate(zip(sources, places))
    ]
    for copy in copies:
        copy.start()
    return copies


def pack_body(*refs):
    count = (len(refs) - 2) // 3
    sources, out_ref, semaphores = refs[:count], refs[count], refs[-1]
    arrived, scratch = refs[count + 1 : 2 * count + 1], refs[2 * count + 1 : -1]
    copies = fetch(sources, arrived, semaphores)
    peers, _, pieces, _ = out_ref.shape
    for i in range(count):
        copies[i].wait()
        channels = arrived[i].shape[0]
        for k in range(pieces):
            lanes = slice(k * LANES, (k + 1) * LANES)
            scratch[i][pl.ds(k, channels, stride=pieces), :] = arrived[i][:, lanes].astype(f32)
        out_ref[:, 2 * i : 2 * i + 2] = scratch[i][...].reshape(peers, 2, pieces, LANES).astype(bf16)


def unpack_body(in_ref, out_ref, scratch):
    channels, length = out_ref.shape
    pieces = length // LANES
    scratch[...] = in_ref[...].astype(f32).reshape(channels * pieces, LANES)
    for k in range(pieces):
        out_ref[:, k * LANES : (k + 1) * LANES] = scratch[pl.ds(k, channels, stride=pieces), :].astype(bf16)


def correlate_body(
    in_ref, long, twiddle, short_hi, short_lo, out_ref, high_ref, low_ref, wide_hi, wide_lo, scratch
):
    waves = wave_of(in_ref, 0), wave_of(in_ref, 2)
    spectra = forward(waves, long, twiddle, short_hi, short_lo, high_ref, low_ref)
    products = []
    for c in range(2):
        s_re, s_im = spectra[c][:, :LANES], spectra[c][:, LANES:]
        g_re, g_im = spectra[2 + c][:, :LANES], spectra[2 + c][:, LANES:]
        products.append((g_re * s_re + g_im * s_im, g_im * s_re - g_re * s_im))
    result = backward(products, long, twiddle, short_hi, short_lo, high_ref, low_ref, wide_hi, wide_lo)
    for c in range(2):
        scratch[pl.ds(c, ROWS, stride=2), :] = result[:, channel_lanes(c)]
    out_ref[...] = scratch[...].astype(bf16).reshape(out_ref.shape)


def adam_body(grad_ref, master, one, two, new_master, new_one, new_two, filters, rounded, semaphores):
    grad = grad_ref[0].astype(f32)
    for q in range(1, grad_ref.shape[0]):
        grad = grad + grad_ref[q].astype(f32)
    first = 0.9 * one[...] + 0.1 * grad
    second = 0.999 * two[...] + 0.001 * grad * grad
    first_hat = first / (1.0 - 0.9**10)
    second_hat = second / (1.0 - 0.999**10)
    old = master[...]
    new = old - 0.01 * (first_hat / (jnp.sqrt(second_hat) + 1e-08) + 0.1 * old)
    rounded[...] = new.astype(bf16)
    owners = filters.shape[0]
    copies = fetch([rounded] * owners, [filters.at[q] for q in range(owners)], semaphores)
    new_one[...] = first
    new_two[...] = second
    new_master[...] = new
    for copy in copies:
        copy.wait()


def spectrum_body(in_ref, long, twiddle, short_hi, short_lo, out_ref, high_ref, low_ref, result, semaphores):
    spectra = forward((wave_of(in_ref, 4),), long, twiddle, short_hi, short_lo, high_ref, low_ref)
    for c in range(2):
        result[channel_rows(c), :] = spectra[c]
    for copy in fetch([result], [out_ref], semaphores):
        copy.wait()


def convolve_body(
    long, in_hbm, next_hbm, twiddle_hbm, short_hi_hbm, short_lo_hbm,
    out_ref, high_ref, low_ref, wide_hi, wide_lo, scratch,
    in_ref, next_ref, twiddle, short_hi, short_lo, semaphores,
):
    copies = fetch(
        (in_hbm, twiddle_hbm, short_hi_hbm, short_lo_hbm, next_hbm),
        (in_ref, twiddle, short_hi, short_lo, next_ref),
        semaphores,
    )
    copies[0].wait()
    scratch[...] = in_ref[...].reshape(2 * ROWS, LANES).astype(f32)
    wave = jnp.concatenate(
        [scratch[pl.ds(c, ROWS, stride=2), :].astype(bf16) for c in range(2)], axis=1
    )
    for copy in copies[1:]:
        copy.wait()
    spectra = forward((wave,), long, twiddle, short_hi, short_lo, high_ref, low_ref)
    products = []
    for c in range(2):
        f_re, f_im = spectra[c][:, :LANES], spectra[c][:, LANES:]
        n_re, n_im = next_ref[channel_rows(c), :LANES], next_ref[channel_rows(c), LANES:]
        products.append((f_re * n_re - f_im * n_im, f_re * n_im + f_im * n_re))
    result = backward(products, long, twiddle, short_hi, short_lo, high_ref, low_ref, wide_hi, wide_lo)
    result = result.astype(bf16)
    peers, pieces = out_ref.shape[0], out_ref.shape[2]
    for c in range(2):
        out_ref[:, c] = result[:, channel_lanes(c)].reshape(peers, pieces, LANES)


def call(body, name, out_shape, scratch, *args, far=(), far_out=False):
    near = [pltpu.with_memory_space_constraint(a, pltpu.VMEM) for a in args]
    far = [pltpu.with_memory_space_constraint(a, pltpu.HBM) for a in far]
    inside, outside = pl.BlockSpec(memory_space=pltpu.VMEM), pl.BlockSpec(memory_space=pltpu.HBM)
    out_specs = [inside] * len(out_shape)
    if far_out:
        out_specs[-1] = outside
        out_shape = (*out_shape[:-1], pltpu.HBM(out_shape[-1].shape, out_shape[-1].dtype))
    return pl.pallas_call(
        body,
        out_shape=out_shape,
        in_specs=[inside] * len(near) + [outside] * len(far),
        out_specs=tuple(out_specs),
        scratch_shapes=scratch,
        name=name,
        compiler_params=pltpu.CompilerParams(vmem_limit_bytes=16 << 20),
    )(*near, *far)


def shape(dims, dtype):
    return jax.ShapeDtypeStruct(dims, dtype)


def interleave(values):
    channels, taps = values.shape
    pieces = taps // LANES
    return values.reshape(channels, pieces, LANES).transpose(1, 0, 2).reshape(channels * pieces, LANES)


def deinterleave(values, channels):
    pieces = values.shape[0] // channels
    return values.reshape(pieces, channels, LANES).transpose(1, 0, 2).reshape(channels, pieces * LANES)


def exchange(values, axis):
    return lax.all_to_all(values, axis, split_axis=0, concat_axis=0, tiled=True)


def local(inputs, out_grad, master, moment_one, moment_two, next_inputs):
    channels, length = inputs.shape[1:]
    peers = lax.axis_size("ctx")
    owners = lax.axis_size("dp")
    pieces = length // LANES
    rows = channels * pieces
    long, twiddle, short_hi, short_lo = (jnp.asarray(t) for t in tables())
    ahead = (long, twiddle, short_hi, short_lo)
    wide = [pltpu.VMEM((2 * ROWS, 2 * LANES), bf16)] * 2
    tall = [pltpu.VMEM((4 * ROWS, 2 * LANES), bf16)] * 2
    narrow = [pltpu.VMEM((2 * ROWS, LANES), f32)]

    sources = (inputs[0], out_grad[0], next_inputs[0])
    (packed,) = call(
        pack_body, "pack", (shape((peers, 6, pieces, LANES), bf16),),
        [pltpu.VMEM((channels, length), bf16)] * 3 + [pltpu.VMEM((rows, LANES), f32)] * 3
        + [pltpu.SemaphoreType.DMA((3,))],
        far=sources,
    )
    waves = exchange(packed, "ctx")
    own = (2 * ROWS // owners, LANES)
    (partial,) = call(
        correlate_body, "correlate", (shape((owners, *own), bf16),), tall + wide + narrow, waves, *ahead
    )
    new_master, new_one, new_two, filters = call(
        adam_body, "adam", (shape(own, f32),) * 3 + (shape((owners, *own), bf16),),
        [pltpu.VMEM(own, bf16), pltpu.SemaphoreType.DMA((owners,))],
        exchange(partial, "dp"), interleave(master), interleave(moment_one), interleave(moment_two), far_out=True,
    )
    spectra = (2 * ROWS, 2 * LANES)
    (next_spectrum,) = call(
        spectrum_body, "spectrum", (shape(spectra, f32),),
        wide + [pltpu.VMEM(spectra, f32), pltpu.SemaphoreType.DMA((1,))], waves, *ahead, far_out=True,
    )
    far = (exchange(filters, "dp"), next_spectrum, twiddle, short_hi, short_lo)
    (result,) = call(
        convolve_body, "convolve", (shape((peers, 2, pieces, LANES), bf16),),
        wide + wide + narrow + [pltpu.VMEM(t.shape, t.dtype) for t in far]
        + [pltpu.SemaphoreType.DMA((len(far),))],
        long, far=far,
    )
    (next_out,) = call(
        unpack_body, "unpack", (shape((channels, length), bf16),), [pltpu.VMEM((rows, LANES), f32)],
        exchange(result, "ctx"),
    )
    return (deinterleave(new_master, 2), deinterleave(new_one, 2), deinterleave(new_two, 2), next_out[None])


def solution(mesh):
    return jax.shard_map(
        local,
        mesh=mesh,
        in_specs=(
            P("dp", None, "ctx"),
            P("dp", None, "ctx"),
            P("ctx", "dp"),
            P("ctx", "dp"),
            P("ctx", "dp"),
            P("dp", None, "ctx"),
        ),
        out_specs=(P("ctx", "dp"), P("ctx", "dp"), P("ctx", "dp"), P("dp", None, "ctx")),
        check_vma=False,
    )
```

```python
import math

import jax
import jax.numpy as jnp
import numpy as np
from jax import lax
from jax.experimental import pallas as pl
from jax.experimental.pallas import tpu as pltpu
from jax.sharding import PartitionSpec as P

ROWS = 512
LANES = 128
BLOCK = 128

f32 = jnp.float32
bf16 = jnp.bfloat16


def split_table(values):
    high = values.astype(bf16)
    low = (values - high.astype(np.float64)).astype(bf16)
    return high, low


def tables():
    half = np.arange(ROWS) + 0.5
    lanes = np.arange(LANES)
    outer = 2.0 * math.pi * np.outer(half, half) / (2 * ROWS)
    long_hi, long_lo = split_table(np.concatenate([np.cos(outer), np.sin(outer)], axis=0))
    turn = 2.0 * math.pi * np.outer(half, lanes / (2.0 * ROWS * LANES) - 1.0 / (4 * ROWS))
    twiddle = np.concatenate([np.cos(turn), np.sin(turn)], axis=1).astype(np.float32)
    inner = 2.0 * math.pi * (np.outer(lanes, lanes) % LANES) / LANES
    cosine, sine = np.cos(inner), np.sin(inner)
    short = np.block([[cosine, sine], [-sine, cosine]])
    short_hi, short_lo = split_table(short)
    fore, rear = slice(0, ROWS // 2), slice(ROWS // 2, ROWS)
    long = np.concatenate([long_hi[:, fore], long_lo[:, fore], -long_hi[:, rear], -long_lo[:, rear]], axis=1)
    return (long, twiddle, short_hi, short_lo)


def dot(left, right):
    return jnp.dot(left, right, preferred_element_type=f32)


def store_halves(values, place, high_ref, low_ref):
    high = values.astype(bf16)
    high_ref[place] = high
    low_ref[place] = (values - high.astype(f32)).astype(bf16)


def times_short(high_ref, low_ref, rows, hi_ref, lo_ref):
    left = jnp.concatenate([high_ref[rows], low_ref[rows], high_ref[rows]], axis=1)
    right = jnp.concatenate([hi_ref[...], hi_ref[...], lo_ref[...]], axis=0)
    return dot(left, right)


def channel_rows(c):
    return slice(c * ROWS, (c + 1) * ROWS)


def channel_lanes(c):
    return slice(c * LANES, (c + 1) * LANES)


def forward(waves, long, twiddle, short_hi, short_lo, high_ref, low_ref, pending=()):
    left, right = slice(0, LANES), slice(LANES, 2 * LANES)
    half = ROWS // 2
    spectra = []
    for wave in waves:
        fore = dot(long[:, :ROWS], jnp.concatenate([wave[:half], wave[:half]], axis=0))
        rear = dot(long[:, ROWS:], jnp.concatenate([wave[half:], wave[half:]], axis=0))
        first = fore - rear
        done = len(spectra)
        for c in range(2):
            at = channel_rows(done + c)
            real, imag = first[:ROWS, channel_lanes(c)], first[ROWS:, channel_lanes(c)]
            cosine, sine = twiddle[:, left], twiddle[:, right]
            store_halves(real * cosine - imag * sine, (at, left), high_ref, low_ref)
            store_halves(real * sine + imag * cosine, (at, right), high_ref, low_ref)
        for copy in pending:
            copy.wait()
        for c in range(2):
            spectra.append(times_short(high_ref, low_ref, channel_rows(done + c), short_hi, short_lo))
    return spectra


def backward(products, long, twiddle, short_hi, short_lo, high_ref, low_ref, wide_hi, wide_lo):
    left, right = slice(0, LANES), slice(LANES, 2 * LANES)
    half = ROWS // 2
    top, end = slice(0, ROWS), slice(ROWS, 2 * ROWS)
    for c, (real, imag) in enumerate(products):
        store_halves(real, (channel_rows(c), left), high_ref, low_ref)
        store_halves(-imag, (channel_rows(c), right), high_ref, low_ref)
    mixed = [
        times_short(high_ref, low_ref, channel_rows(c), short_hi, short_lo) for c in range(len(products))
    ]
    for c in range(len(products)):
        cosine, sine = twiddle[:, left], twiddle[:, right]
        mixed_re, mixed_im = mixed[c][:, left], mixed[c][:, right]
        store_halves(mixed_re * cosine - mixed_im * sine, (top, channel_lanes(c)), wide_hi, wide_lo)
        store_halves(-(mixed_im * cosine + mixed_re * sine), (end, channel_lanes(c)), wide_hi, wide_lo)
    total = []
    for at in (0, half):
        both, high = slice(2 * at, 2 * at + ROWS), slice(2 * at, 2 * at + half)
        real, imag = slice(at, at + half), slice(ROWS + at, ROWS + at + half)
        table = jnp.concatenate([long[top, both], long[end, both], long[top, high], long[end, high]], axis=1)
        waves = [wide_hi[real], wide_hi[real], wide_hi[imag], wide_hi[imag], wide_lo[real], wide_lo[imag]]
        total.append(dot(table, jnp.concatenate(waves, axis=0)))
    return (total[0] - total[1]) * (1.0 / (ROWS * LANES))


def wave_of(ref, first):
    parts = [ref[:, first + c].reshape(ROWS, LANES) for c in range(2)]
    return jnp.concatenate(parts, axis=1)


def fetch(sources, places, semaphores):
    copies = [
        pltpu.make_async_copy(source, place, semaphores.at[i])
        for i, (source, place) in enumerate(zip(sources, places))
    ]
    for copy in copies:
        copy.start()
    return copies


def pack_body(*refs):
    count = (len(refs) - 2) // 3
    sources, out_ref, semaphores = refs[:count], refs[count], refs[-1]
    arrived, scratch = refs[count + 1 : 2 * count + 1], refs[2 * count + 1 : -1]
    copies = fetch(sources, arrived, semaphores)
    peers, _, pieces, _ = out_ref.shape
    for i in range(count):
        copies[i].wait()
        channels = arrived[i].shape[0]
        for k in range(pieces):
            lanes = slice(k * LANES, (k + 1) * LANES)
            scratch[i][pl.ds(k, channels, stride=pieces), :] = arrived[i][:, lanes].astype(f32)
        out_ref[:, 2 * i : 2 * i + 2] = scratch[i][...].reshape(peers, 2, pieces, LANES).astype(bf16)


def unpack_body(in_ref, out_ref, scratch):
    channels, length = out_ref.shape
    pieces = length // LANES
    scratch[...] = in_ref[...].astype(f32).reshape(channels * pieces, LANES)
    for k in range(pieces):
        out_ref[:, k * LANES : (k + 1) * LANES] = scratch[pl.ds(k, channels, stride=pieces), :].astype(bf16)


def correlate_body(
    in_ref, long, twiddle, short_hi, short_lo, out_ref, next_hbm,
    high_ref, low_ref, wide_hi, wide_lo, scratch, next_spectra, semaphores,
):
    waves = [wave_of(in_ref, 2 * i) for i in range(3)]
    spectra = forward(waves, long, twiddle, short_hi, short_lo, high_ref, low_ref)
    for c in range(2):
        next_spectra[channel_rows(c), :] = spectra[4 + c]
    copies = fetch([next_spectra], [next_hbm], semaphores)
    products = []
    for c in range(2):
        s_re, s_im = spectra[c][:, :LANES], spectra[c][:, LANES:]
        g_re, g_im = spectra[2 + c][:, :LANES], spectra[2 + c][:, LANES:]
        products.append((g_re * s_re + g_im * s_im, g_im * s_re - g_re * s_im))
    result = backward(products, long, twiddle, short_hi, short_lo, high_ref, low_ref, wide_hi, wide_lo)
    for c in range(2):
        scratch[pl.ds(c, ROWS, stride=2), :] = result[:, channel_lanes(c)]
    out_ref[...] = scratch[...].astype(bf16).reshape(out_ref.shape)
    copies[0].wait()


def adam_body(grad_ref, master, one, two, new_master, new_one, new_two, filters):
    grad = grad_ref[0].astype(f32)
    for q in range(1, grad_ref.shape[0]):
        grad = grad + grad_ref[q].astype(f32)
    first = 0.9 * one[...] + 0.1 * grad
    second = 0.999 * two[...] + 0.001 * grad * grad
    first_hat = first / (1.0 - 0.9**10)
    second_hat = second / (1.0 - 0.999**10)
    old = master[...]
    new = old - 0.01 * (first_hat / (jnp.sqrt(second_hat) + 1e-08) + 0.1 * old)
    new_one[...] = first
    new_two[...] = second
    new_master[...] = new
    rounded = new.astype(bf16)
    for q in range(filters.shape[0]):
        filters[q] = rounded


def convolve_body(
    in_ref, long, twiddle, short_hi, short_lo, next_hbm,
    out_ref, high_ref, low_ref, wide_hi, wide_lo, scratch, next_ref, semaphores,
):
    copies = fetch([next_hbm], [next_ref], semaphores)
    scratch[...] = in_ref[...].reshape(2 * ROWS, LANES).astype(f32)
    wave = jnp.concatenate(
        [scratch[pl.ds(c, ROWS, stride=2), :].astype(bf16) for c in range(2)], axis=1
    )
    spectra = forward((wave,), long, twiddle, short_hi, short_lo, high_ref, low_ref, copies)
    products = []
    for c in range(2):
        f_re, f_im = spectra[c][:, :LANES], spectra[c][:, LANES:]
        n_re, n_im = next_ref[channel_rows(c), :LANES], next_ref[channel_rows(c), LANES:]
        products.append((f_re * n_re - f_im * n_im, f_re * n_im + f_im * n_re))
    result = backward(products, long, twiddle, short_hi, short_lo, high_ref, low_ref, wide_hi, wide_lo)
    result = result.astype(bf16)
    peers, pieces = out_ref.shape[0], out_ref.shape[2]
    for c in range(2):
        out_ref[:, c] = result[:, channel_lanes(c)].reshape(peers, pieces, LANES)


def call(body, name, out_shape, scratch, *args, far=(), far_out=False):
    near = [pltpu.with_memory_space_constraint(a, pltpu.VMEM) for a in args]
    far = [pltpu.with_memory_space_constraint(a, pltpu.HBM) for a in far]
    inside, outside = pl.BlockSpec(memory_space=pltpu.VMEM), pl.BlockSpec(memory_space=pltpu.HBM)
    out_specs = [inside] * len(out_shape)
    if far_out:
        out_specs[-1] = outside
        out_shape = (*out_shape[:-1], pltpu.HBM(out_shape[-1].shape, out_shape[-1].dtype))
    return pl.pallas_call(
        body,
        out_shape=out_shape,
        in_specs=[inside] * len(near) + [outside] * len(far),
        out_specs=tuple(out_specs),
        scratch_shapes=scratch,
        name=name,
        compiler_params=pltpu.CompilerParams(vmem_limit_bytes=16 << 20),
    )(*near, *far)


def shape(dims, dtype):
    return jax.ShapeDtypeStruct(dims, dtype)


def interleave(values):
    channels, taps = values.shape
    pieces = taps // LANES
    return values.reshape(channels, pieces, LANES).transpose(1, 0, 2).reshape(channels * pieces, LANES)


def deinterleave(values, channels):
    pieces = values.shape[0] // channels
    return values.reshape(pieces, channels, LANES).transpose(1, 0, 2).reshape(channels, pieces * LANES)


def exchange(values, axis):
    return lax.all_to_all(values, axis, split_axis=0, concat_axis=0, tiled=True)


def local(inputs, out_grad, master, moment_one, moment_two, next_inputs):
    channels, length = inputs.shape[1:]
    peers = lax.axis_size("ctx")
    owners = lax.axis_size("dp")
    pieces = length // LANES
    rows = channels * pieces
    long, twiddle, short_hi, short_lo = (jnp.asarray(t) for t in tables())
    ahead = (long, twiddle, short_hi, short_lo)
    wide = [pltpu.VMEM((2 * ROWS, 2 * LANES), bf16)] * 2
    narrow = [pltpu.VMEM((2 * ROWS, LANES), f32)]

    sources = (inputs[0], out_grad[0], next_inputs[0])
    (packed,) = call(
        pack_body, "pack", (shape((peers, 6, pieces, LANES), bf16),),
        [pltpu.VMEM((channels, length), bf16)] * 3 + [pltpu.VMEM((rows, LANES), f32)] * 3
        + [pltpu.SemaphoreType.DMA((3,))],
        far=sources,
    )
    own = (2 * ROWS // owners, LANES)
    spectra = (2 * ROWS, 2 * LANES)
    partial, next_spectrum = call(
        correlate_body, "correlate", (shape((owners, *own), bf16), shape(spectra, f32)),
        [pltpu.VMEM((6 * ROWS, 2 * LANES), bf16)] * 2 + wide + narrow
        + [pltpu.VMEM(spectra, f32), pltpu.SemaphoreType.DMA((1,))],
        exchange(packed, "ctx"), *ahead, far_out=True,
    )
    new_master, new_one, new_two, filters = call(
        adam_body, "adam", (shape(own, f32),) * 3 + (shape((owners, *own), bf16),), [],
        exchange(partial, "dp"), interleave(master), interleave(moment_one), interleave(moment_two),
    )
    (result,) = call(
        convolve_body, "convolve", (shape((peers, 2, pieces, LANES), bf16),),
        wide + wide + narrow + [pltpu.VMEM(spectra, f32), pltpu.SemaphoreType.DMA((1,))],
        exchange(filters, "dp"), *ahead, far=(next_spectrum,),
    )
    (next_out,) = call(
        unpack_body, "unpack", (shape((channels, length), bf16),), [pltpu.VMEM((rows, LANES), f32)],
        exchange(result, "ctx"),
    )
    return (deinterleave(new_master, 2), deinterleave(new_one, 2), deinterleave(new_two, 2), next_out[None])


def solution(mesh):
    return jax.shard_map(
        local,
        mesh=mesh,
        in_specs=(
            P("dp", None, "ctx"),
            P("dp", None, "ctx"),
            P("ctx", "dp"),
            P("ctx", "dp"),
            P("ctx", "dp"),
            P("dp", None, "ctx"),
        ),
        out_specs=(P("ctx", "dp"), P("ctx", "dp"), P("ctx", "dp"), P("dp", None, "ctx")),
        check_vma=False,
    )
```

```python
import math

import jax
import jax.numpy as jnp
import numpy as np
from jax import lax
from jax.experimental import pallas as pl
from jax.experimental.pallas import tpu as pltpu
from jax.sharding import PartitionSpec as P

ROWS = 512
LANES = 128
BLOCK = 128

f32 = jnp.float32
bf16 = jnp.bfloat16


def split_table(values):
    high = values.astype(bf16)
    low = (values - high.astype(np.float64)).astype(bf16)
    return high, low


def tables():
    half = np.arange(ROWS) + 0.5
    lanes = np.arange(LANES)
    outer = 2.0 * math.pi * np.outer(half, half) / (2 * ROWS)
    long_hi, long_lo = split_table(np.concatenate([np.cos(outer), np.sin(outer)], axis=0))
    turn = 2.0 * math.pi * np.outer(half, lanes / (2.0 * ROWS * LANES) - 1.0 / (4 * ROWS))
    twiddle = np.concatenate([np.cos(turn), np.sin(turn)], axis=1).astype(np.float32)
    inner = 2.0 * math.pi * (np.outer(lanes, lanes) % LANES) / LANES
    cosine, sine = np.cos(inner), np.sin(inner)
    short = np.block([[cosine, sine], [-sine, cosine]])
    short_hi, short_lo = split_table(short)
    fore, rear = slice(0, ROWS // 2), slice(ROWS // 2, ROWS)
    long = np.concatenate([long_hi[:, fore], long_lo[:, fore], -long_hi[:, rear], -long_lo[:, rear]], axis=1)
    return (long, twiddle, short_hi, short_lo)


def dot(left, right):
    return jnp.dot(left, right, preferred_element_type=f32)


def store_halves(values, place, high_ref, low_ref):
    high = values.astype(bf16)
    high_ref[place] = high
    low_ref[place] = (values - high.astype(f32)).astype(bf16)


def times_short(high_ref, low_ref, rows, hi_ref, lo_ref):
    left = jnp.concatenate([high_ref[rows], low_ref[rows], high_ref[rows]], axis=1)
    right = jnp.concatenate([hi_ref[...], hi_ref[...], lo_ref[...]], axis=0)
    return dot(left, right)


def channel_rows(c):
    return slice(c * ROWS, (c + 1) * ROWS)


def channel_lanes(c):
    return slice(c * LANES, (c + 1) * LANES)


def forward(waves, long, twiddle, short_hi, short_lo, high_ref, low_ref, pending=()):
    left, right = slice(0, LANES), slice(LANES, 2 * LANES)
    half = ROWS // 2
    spectra = []
    firsts = []
    for wave in waves:
        fore = dot(long[:, :ROWS], jnp.concatenate([wave[:half], wave[:half]], axis=0))
        rear = dot(long[:, ROWS:], jnp.concatenate([wave[half:], wave[half:]], axis=0))
        firsts.append(fore - rear)
    for w, first in enumerate(firsts):
        for c in range(2):
            at = channel_rows(2 * w + c)
            real, imag = first[:ROWS, channel_lanes(c)], first[ROWS:, channel_lanes(c)]
            cosine, sine = twiddle[:, left], twiddle[:, right]
            store_halves(real * cosine - imag * sine, (at, left), high_ref, low_ref)
            store_halves(real * sine + imag * cosine, (at, right), high_ref, low_ref)
    for copy in pending:
        copy.wait()
    for w in range(len(waves)):
        for c in range(2):
            spectra.append(times_short(high_ref, low_ref, channel_rows(2 * w + c), short_hi, short_lo))
    return spectra


def backward(products, long, twiddle, short_hi, short_lo, high_ref, low_ref, wide_hi, wide_lo):
    left, right = slice(0, LANES), slice(LANES, 2 * LANES)
    half = ROWS // 2
    top, end = slice(0, ROWS), slice(ROWS, 2 * ROWS)
    for c, (real, imag) in enumerate(products):
        store_halves(real, (channel_rows(c), left), high_ref, low_ref)
        store_halves(-imag, (channel_rows(c), right), high_ref, low_ref)
    mixed = [
        times_short(high_ref, low_ref, channel_rows(c), short_hi, short_lo) for c in range(len(products))
    ]
    for c in range(len(products)):
        cosine, sine = twiddle[:, left], twiddle[:, right]
        mixed_re, mixed_im = mixed[c][:, left], mixed[c][:, right]
        store_halves(mixed_re * cosine - mixed_im * sine, (top, channel_lanes(c)), wide_hi, wide_lo)
        store_halves(-(mixed_im * cosine + mixed_re * sine), (end, channel_lanes(c)), wide_hi, wide_lo)
    total = []
    for at in (0, half):
        both, high = slice(2 * at, 2 * at + ROWS), slice(2 * at, 2 * at + half)
        real, imag = slice(at, at + half), slice(ROWS + at, ROWS + at + half)
        table = jnp.concatenate([long[top, both], long[end, both], long[top, high], long[end, high]], axis=1)
        waves = [wide_hi[real], wide_hi[real], wide_hi[imag], wide_hi[imag], wide_lo[real], wide_lo[imag]]
        total.append(dot(table, jnp.concatenate(waves, axis=0)))
    return (total[0] - total[1]) * (1.0 / (ROWS * LANES))


def wave_of(ref, first):
    parts = [ref[:, first + c].reshape(ROWS, LANES) for c in range(2)]
    return jnp.concatenate(parts, axis=1)


def fetch(sources, places, semaphores):
    copies = [
        pltpu.make_async_copy(source, place, semaphores.at[i])
        for i, (source, place) in enumerate(zip(sources, places))
    ]
    for copy in copies:
        copy.start()
    return copies


def pack_body(*refs):
    count = (len(refs) - 2) // 3
    sources, out_ref, semaphores = refs[:count], refs[count], refs[-1]
    arrived, scratch = refs[count + 1 : 2 * count + 1], refs[2 * count + 1 : -1]
    copies = fetch(sources, arrived, semaphores)
    peers, _, pieces, _ = out_ref.shape
    for i in range(count):
        copies[i].wait()
        channels = arrived[i].shape[0]
        pitch = pieces + 1
        for k in range(pieces):
            lanes = slice(k * LANES, (k + 1) * LANES)
            scratch[i][pl.ds(k, channels, stride=pitch), :] = arrived[i][:, lanes].astype(f32)
        for c in range(channels):
            out_ref[c // 2, 2 * i + c % 2] = scratch[i][c * pitch : c * pitch + pieces, :].astype(bf16)


def unpack_body(in_ref, out_hbm, scratch, result, semaphores):
    channels, length = out_hbm.shape
    pieces = length // LANES
    pitch = pieces + 1
    group = 16
    copies = []
    for start in range(0, channels, group):
        for c in range(start, start + group):
            scratch[c * pitch : c * pitch + pieces, :] = in_ref[c // 2, c % 2].astype(f32)
        rows = pl.ds(start, group)
        for k in range(pieces):
            lanes = slice(k * LANES, (k + 1) * LANES)
            result[rows, lanes] = scratch[pl.ds(start * pitch + k, group, stride=pitch), :].astype(bf16)
        copies += fetch([result.at[rows]], [out_hbm.at[rows]], semaphores.at[pl.ds(start // group, 1)])
    for copy in copies:
        copy.wait()


def correlate_body(
    in_ref, long, twiddle, short_hi, short_lo, out_ref, next_hbm,
    high_ref, low_ref, wide_hi, wide_lo, scratch, next_spectra, semaphores,
):
    waves = [wave_of(in_ref, 2 * i) for i in range(3)]
    spectra = forward(waves, long, twiddle, short_hi, short_lo, high_ref, low_ref)
    for c in range(2):
        next_spectra[channel_rows(c), :] = spectra[4 + c]
    copies = fetch([next_spectra], [next_hbm], semaphores)
    products = []
    for c in range(2):
        s_re, s_im = spectra[c][:, :LANES], spectra[c][:, LANES:]
        g_re, g_im = spectra[2 + c][:, :LANES], spectra[2 + c][:, LANES:]
        products.append((g_re * s_re + g_im * s_im, g_im * s_re - g_re * s_im))
    result = backward(products, long, twiddle, short_hi, short_lo, high_ref, low_ref, wide_hi, wide_lo)
    for c in range(2):
        scratch[pl.ds(c, ROWS, stride=2), :] = result[:, channel_lanes(c)]
    out_ref[...] = scratch[...].astype(bf16).reshape(out_ref.shape)
    copies[0].wait()


def adam_body(grad_ref, master, one, two, new_master, new_one, new_two, filters):
    grad = grad_ref[0].astype(f32)
    for q in range(1, grad_ref.shape[0]):
        grad = grad + grad_ref[q].astype(f32)
    first = 0.9 * one[...] + 0.1 * grad
    second = 0.999 * two[...] + 0.001 * grad * grad
    first_hat = first / (1.0 - 0.9**10)
    second_hat = second / (1.0 - 0.999**10)
    old = master[...]
    new = old - 0.01 * (first_hat / (jnp.sqrt(second_hat) + 1e-08) + 0.1 * old)
    new_one[...] = first
    new_two[...] = second
    new_master[...] = new
    rounded = new.astype(bf16)
    for q in range(filters.shape[0]):
        filters[q] = rounded


def convolve_body(
    in_ref, long, twiddle, short_hi, short_lo, next_hbm,
    out_ref, high_ref, low_ref, wide_hi, wide_lo, scratch, next_ref, semaphores,
):
    copies = fetch([next_hbm], [next_ref], semaphores)
    scratch[...] = in_ref[...].reshape(2 * ROWS, LANES).astype(f32)
    wave = jnp.concatenate(
        [scratch[pl.ds(c, ROWS, stride=2), :].astype(bf16) for c in range(2)], axis=1
    )
    spectra = forward((wave,), long, twiddle, short_hi, short_lo, high_ref, low_ref, copies)
    products = []
    for c in range(2):
        f_re, f_im = spectra[c][:, :LANES], spectra[c][:, LANES:]
        n_re, n_im = next_ref[channel_rows(c), :LANES], next_ref[channel_rows(c), LANES:]
        products.append((f_re * n_re - f_im * n_im, f_re * n_im + f_im * n_re))
    result = backward(products, long, twiddle, short_hi, short_lo, high_ref, low_ref, wide_hi, wide_lo)
    result = result.astype(bf16)
    peers, pieces = out_ref.shape[0], out_ref.shape[2]
    for c in range(2):
        out_ref[:, c] = result[:, channel_lanes(c)].reshape(peers, pieces, LANES)


def call(body, name, out_shape, scratch, *args, far=(), far_out=False):
    near = [pltpu.with_memory_space_constraint(a, pltpu.VMEM) for a in args]
    far = [pltpu.with_memory_space_constraint(a, pltpu.HBM) for a in far]
    inside, outside = pl.BlockSpec(memory_space=pltpu.VMEM), pl.BlockSpec(memory_space=pltpu.HBM)
    out_specs = [inside] * len(out_shape)
    if far_out:
        out_specs[-1] = outside
        out_shape = (*out_shape[:-1], pltpu.HBM(out_shape[-1].shape, out_shape[-1].dtype))
    return pl.pallas_call(
        body,
        out_shape=out_shape,
        in_specs=[inside] * len(near) + [outside] * len(far),
        out_specs=tuple(out_specs),
        scratch_shapes=scratch,
        name=name,
        compiler_params=pltpu.CompilerParams(vmem_limit_bytes=16 << 20),
    )(*near, *far)


def shape(dims, dtype):
    return jax.ShapeDtypeStruct(dims, dtype)


def interleave(values):
    channels, taps = values.shape
    pieces = taps // LANES
    return values.reshape(channels, pieces, LANES).transpose(1, 0, 2).reshape(channels * pieces, LANES)


def deinterleave(values, channels):
    pieces = values.shape[0] // channels
    return values.reshape(pieces, channels, LANES).transpose(1, 0, 2).reshape(channels, pieces * LANES)


def exchange(values, axis):
    return lax.all_to_all(values, axis, split_axis=0, concat_axis=0, tiled=True)


def local(inputs, out_grad, master, moment_one, moment_two, next_inputs):
    channels, length = inputs.shape[1:]
    peers = lax.axis_size("ctx")
    owners = lax.axis_size("dp")
    pieces = length // LANES
    rows = channels * pieces
    long, twiddle, short_hi, short_lo = (jnp.asarray(t) for t in tables())
    ahead = (long, twiddle, short_hi, short_lo)
    wide = [pltpu.VMEM((2 * ROWS, 2 * LANES), bf16)] * 2
    narrow = [pltpu.VMEM((2 * ROWS, LANES), f32)]

    sources = (inputs[0], out_grad[0], next_inputs[0])
    (packed,) = call(
        pack_body, "pack", (shape((peers, 6, pieces, LANES), bf16),),
        [pltpu.VMEM((channels, length), bf16)] * 3 + [pltpu.VMEM((rows + channels, LANES), f32)] * 3
        + [pltpu.SemaphoreType.DMA((3,))],
        far=sources,
    )
    own = (2 * ROWS // owners, LANES)
    spectra = (2 * ROWS, 2 * LANES)
    partial, next_spectrum = call(
        correlate_body, "correlate", (shape((owners, *own), bf16), shape(spectra, f32)),
        [pltpu.VMEM((6 * ROWS, 2 * LANES), bf16)] * 2 + wide + narrow
        + [pltpu.VMEM(spectra, f32), pltpu.SemaphoreType.DMA((1,))],
        exchange(packed, "ctx"), *ahead, far_out=True,
    )
    new_master, new_one, new_two, filters = call(
        adam_body, "adam", (shape(own, f32),) * 3 + (shape((owners, *own), bf16),), [],
        exchange(partial, "dp"), interleave(master), interleave(moment_one), interleave(moment_two),
    )
    (result,) = call(
        convolve_body, "convolve", (shape((peers, 2, pieces, LANES), bf16),),
        wide + wide + narrow + [pltpu.VMEM(spectra, f32), pltpu.SemaphoreType.DMA((1,))],
        exchange(filters, "dp"), *ahead, far=(next_spectrum,),
    )
    (next_out,) = call(
        unpack_body, "unpack", (shape((channels, length), bf16),),
        [pltpu.VMEM((rows + channels, LANES), f32), pltpu.VMEM((channels, length), bf16)]
        + [pltpu.SemaphoreType.DMA((channels // 16,))],
        exchange(result, "ctx"), far_out=True,
    )
    return (deinterleave(new_master, 2), deinterleave(new_one, 2), deinterleave(new_two, 2), next_out[None])


def solution(mesh):
    return jax.shard_map(
        local,
        mesh=mesh,
        in_specs=(
            P("dp", None, "ctx"),
            P("dp", None, "ctx"),
            P("ctx", "dp"),
            P("ctx", "dp"),
            P("ctx", "dp"),
            P("dp", None, "ctx"),
        ),
        out_specs=(P("ctx", "dp"), P("ctx", "dp"), P("ctx", "dp"), P("dp", None, "ctx")),
        check_vma=False,
    )
```

```python
import math

import jax
import jax.numpy as jnp
import numpy as np
from jax import lax
from jax.experimental import pallas as pl
from jax.experimental.pallas import tpu as pltpu
from jax.sharding import PartitionSpec as P

ROWS = 512
LANES = 128
BLOCK = 128

f32 = jnp.float32
bf16 = jnp.bfloat16


def split_table(values):
    high = values.astype(bf16)
    low = (values - high.astype(np.float64)).astype(bf16)
    return high, low


def tables():
    half = np.arange(ROWS) + 0.5
    lanes = np.arange(LANES)
    outer = 2.0 * math.pi * np.outer(half, half) / (2 * ROWS)
    long_hi, long_lo = split_table(np.concatenate([np.cos(outer), np.sin(outer)], axis=0))
    turn = 2.0 * math.pi * np.outer(half, lanes / (2.0 * ROWS * LANES) - 1.0 / (4 * ROWS))
    twiddle = np.concatenate([np.cos(turn), np.sin(turn)], axis=1).astype(np.float32)
    inner = 2.0 * math.pi * (np.outer(lanes, lanes) % LANES) / LANES
    cosine, sine = np.cos(inner), np.sin(inner)
    short = np.block([[cosine, sine], [-sine, cosine]])
    short_hi, short_lo = split_table(short)
    fore, rear = slice(0, ROWS // 2), slice(ROWS // 2, ROWS)
    long = np.concatenate([long_hi[:, fore], long_lo[:, fore], -long_hi[:, rear], -long_lo[:, rear]], axis=1)
    return (long, twiddle, short_hi, short_lo)


def dot(left, right):
    return jnp.dot(left, right, preferred_element_type=f32)


def store_halves(values, place, high_ref, low_ref):
    high = values.astype(bf16)
    high_ref[place] = high
    low_ref[place] = (values - high.astype(f32)).astype(bf16)


def times_short(high_ref, low_ref, rows, hi_ref, lo_ref):
    left = jnp.concatenate([high_ref[rows], low_ref[rows], high_ref[rows]], axis=1)
    right = jnp.concatenate([hi_ref[...], hi_ref[...], lo_ref[...]], axis=0)
    return dot(left, right)


def channel_rows(c):
    return slice(c * ROWS, (c + 1) * ROWS)


def channel_lanes(c):
    return slice(c * LANES, (c + 1) * LANES)


LEFT, RIGHT = slice(0, LANES), slice(LANES, 2 * LANES)


def first_stage(wave, long):
    half = ROWS // 2
    fore = dot(long[:, :ROWS], jnp.concatenate([wave[:half], wave[:half]], axis=0))
    rear = dot(long[:, ROWS:], jnp.concatenate([wave[half:], wave[half:]], axis=0))
    return fore - rear


def turn(first, c, slot, twiddle, high_ref, low_ref):
    at = channel_rows(slot)
    real, imag = first[:ROWS, channel_lanes(c)], first[ROWS:, channel_lanes(c)]
    cosine, sine = twiddle[:, LEFT], twiddle[:, RIGHT]
    store_halves(real * cosine - imag * sine, (at, LEFT), high_ref, low_ref)
    store_halves(real * sine + imag * cosine, (at, RIGHT), high_ref, low_ref)


def mix(product, slot, short_hi, short_lo, high_ref, low_ref):
    store_halves(product[0], (channel_rows(slot), LEFT), high_ref, low_ref)
    store_halves(product[1], (channel_rows(slot), RIGHT), high_ref, low_ref)
    return times_short(high_ref, low_ref, channel_rows(slot), short_hi, short_lo)


def turn_back(mixed, c, twiddle, wide_hi, wide_lo):
    cosine, sine = twiddle[:, LEFT], twiddle[:, RIGHT]
    real, imag = mixed[:, LEFT], mixed[:, RIGHT]
    top, end = slice(0, ROWS), slice(ROWS, 2 * ROWS)
    store_halves(real * cosine - imag * sine, (top, channel_lanes(c)), wide_hi, wide_lo)
    store_halves(-(imag * cosine + real * sine), (end, channel_lanes(c)), wide_hi, wide_lo)


def last_stage(long, wide_hi, wide_lo):
    half = ROWS // 2
    top, end = slice(0, ROWS), slice(ROWS, 2 * ROWS)
    total = []
    for at in (0, half):
        both, high = slice(2 * at, 2 * at + ROWS), slice(2 * at, 2 * at + half)
        real, imag = slice(at, at + half), slice(ROWS + at, ROWS + at + half)
        table = jnp.concatenate([long[top, both], long[end, both], long[top, high], long[end, high]], axis=1)
        waves = [wide_hi[real], wide_hi[real], wide_hi[imag], wide_hi[imag], wide_lo[real], wide_lo[imag]]
        total.append(dot(table, jnp.concatenate(waves, axis=0)))
    return (total[0] - total[1]) * (1.0 / (ROWS * LANES))


def wave_of(ref, first):
    parts = [ref[:, first + c].reshape(ROWS, LANES) for c in range(2)]
    return jnp.concatenate(parts, axis=1)


def fetch(sources, places, semaphores):
    copies = [
        pltpu.make_async_copy(source, place, semaphores.at[i])
        for i, (source, place) in enumerate(zip(sources, places))
    ]
    for copy in copies:
        copy.start()
    return copies


def pack_body(*refs):
    count = (len(refs) - 2) // 3
    sources, out_ref, semaphores = refs[:count], refs[count], refs[-1]
    arrived, scratch = refs[count + 1 : 2 * count + 1], refs[2 * count + 1 : -1]
    copies = fetch(sources, arrived, semaphores)
    peers, _, pieces, _ = out_ref.shape
    for i in range(count):
        copies[i].wait()
        channels = arrived[i].shape[0]
        pitch = pieces + 1
        for k in range(pieces):
            lanes = slice(k * LANES, (k + 1) * LANES)
            scratch[i][pl.ds(k, channels, stride=pitch), :] = arrived[i][:, lanes].astype(f32)
        for c in range(channels):
            out_ref[c // 2, 2 * i + c % 2] = scratch[i][c * pitch : c * pitch + pieces, :].astype(bf16)


def unpack_body(in_ref, out_hbm, scratch, result, semaphores):
    channels, length = out_hbm.shape
    pieces = length // LANES
    pitch = pieces + 1
    group = 16
    copies = []
    for start in range(0, channels, group):
        for c in range(start, start + group):
            scratch[c * pitch : c * pitch + pieces, :] = in_ref[c // 2, c % 2].astype(f32)
        rows = pl.ds(start, group)
        for k in range(pieces):
            lanes = slice(k * LANES, (k + 1) * LANES)
            result[rows, lanes] = scratch[pl.ds(start * pitch + k, group, stride=pitch), :].astype(bf16)
        copies += fetch([result.at[rows]], [out_hbm.at[rows]], semaphores.at[pl.ds(start // group, 1)])
    for copy in copies:
        copy.wait()


def correlate_body(
    in_ref, long, twiddle, short_hi, short_lo, out_ref, next_hbm,
    high_ref, low_ref, wide_hi, wide_lo, scratch, next_spectra, semaphores,
):
    firsts = [first_stage(wave_of(in_ref, 2 * i), long) for i in range(3)]
    for c in range(2):
        spectra = []
        for w in range(2):
            turn(firsts[w], c, 3 * c + w, twiddle, high_ref, low_ref)
            spectra.append(times_short(high_ref, low_ref, channel_rows(3 * c + w), short_hi, short_lo))
        (s_re, s_im), (g_re, g_im) = [(t[:, LEFT], t[:, RIGHT]) for t in spectra]
        turn(firsts[2], c, 3 * c + 2, twiddle, high_ref, low_ref)
        next_spectra[channel_rows(c), :] = times_short(
            high_ref, low_ref, channel_rows(3 * c + 2), short_hi, short_lo
        )
        product = (g_re * s_re + g_im * s_im, g_re * s_im - g_im * s_re)
        mixed = mix(product, 3 * c, short_hi, short_lo, high_ref, low_ref)
        turn_back(mixed, c, twiddle, wide_hi, wide_lo)
    copies = fetch([next_spectra], [next_hbm], semaphores)
    result = last_stage(long, wide_hi, wide_lo)
    for c in range(2):
        scratch[pl.ds(c, ROWS, stride=2), :] = result[:, channel_lanes(c)]
    out_ref[...] = scratch[...].astype(bf16).reshape(out_ref.shape)
    copies[0].wait()


def adam_body(grad_ref, master, one, two, new_master, new_one, new_two, filters):
    grad = grad_ref[0].astype(f32)
    for q in range(1, grad_ref.shape[0]):
        grad = grad + grad_ref[q].astype(f32)
    first = 0.9 * one[...] + 0.1 * grad
    second = 0.999 * two[...] + 0.001 * grad * grad
    first_hat = first / (1.0 - 0.9**10)
    second_hat = second / (1.0 - 0.999**10)
    old = master[...]
    new = old - 0.01 * (first_hat / (jnp.sqrt(second_hat) + 1e-08) + 0.1 * old)
    new_one[...] = first
    new_two[...] = second
    new_master[...] = new
    rounded = new.astype(bf16)
    for q in range(filters.shape[0]):
        filters[q] = rounded


def convolve_body(
    in_ref, long, twiddle, short_hi, short_lo, next_hbm,
    out_ref, high_ref, low_ref, wide_hi, wide_lo, scratch, next_ref, semaphores,
):
    copies = fetch([next_hbm], [next_ref], semaphores)
    scratch[...] = in_ref[...].reshape(2 * ROWS, LANES).astype(f32)
    wave = jnp.concatenate(
        [scratch[pl.ds(c, ROWS, stride=2), :].astype(bf16) for c in range(2)], axis=1
    )
    first = first_stage(wave, long)
    for c in range(2):
        turn(first, c, c, twiddle, high_ref, low_ref)
    copies[0].wait()
    spectra = [times_short(high_ref, low_ref, channel_rows(c), short_hi, short_lo) for c in range(2)]
    mixed = []
    for c in range(2):
        f_re, f_im = spectra[c][:, LEFT], spectra[c][:, RIGHT]
        n_re, n_im = next_ref[channel_rows(c), LEFT], next_ref[channel_rows(c), RIGHT]
        product = (f_re * n_re - f_im * n_im, -(f_re * n_im + f_im * n_re))
        mixed.append(mix(product, c, short_hi, short_lo, high_ref, low_ref))
    for c in range(2):
        turn_back(mixed[c], c, twiddle, wide_hi, wide_lo)
    result = last_stage(long, wide_hi, wide_lo)
    result = result.astype(bf16)
    peers, pieces = out_ref.shape[0], out_ref.shape[2]
    for c in range(2):
        out_ref[:, c] = result[:, channel_lanes(c)].reshape(peers, pieces, LANES)


def call(body, name, out_shape, scratch, *args, far=(), far_out=False, flags=None):
    near = [pltpu.with_memory_space_constraint(a, pltpu.VMEM) for a in args]
    far = [pltpu.with_memory_space_constraint(a, pltpu.HBM) for a in far]
    inside, outside = pl.BlockSpec(memory_space=pltpu.VMEM), pl.BlockSpec(memory_space=pltpu.HBM)
    out_specs = [inside] * len(out_shape)
    if far_out:
        out_specs[-1] = outside
        out_shape = (*out_shape[:-1], pltpu.HBM(out_shape[-1].shape, out_shape[-1].dtype))
    return pl.pallas_call(
        body,
        out_shape=out_shape,
        in_specs=[inside] * len(near) + [outside] * len(far),
        out_specs=tuple(out_specs),
        scratch_shapes=scratch,
        name=name,
        compiler_params=pltpu.CompilerParams(vmem_limit_bytes=16 << 20, flags=flags),
    )(*near, *far)


def shape(dims, dtype):
    return jax.ShapeDtypeStruct(dims, dtype)


def interleave(values):
    channels, taps = values.shape
    pieces = taps // LANES
    return values.reshape(channels, pieces, LANES).transpose(1, 0, 2).reshape(channels * pieces, LANES)


def deinterleave(values, channels):
    pieces = values.shape[0] // channels
    return values.reshape(pieces, channels, LANES).transpose(1, 0, 2).reshape(channels, pieces * LANES)


def exchange(values, axis):
    return lax.all_to_all(values, axis, split_axis=0, concat_axis=0, tiled=True)


def local(inputs, out_grad, master, moment_one, moment_two, next_inputs):
    channels, length = inputs.shape[1:]
    peers = lax.axis_size("ctx")
    owners = lax.axis_size("dp")
    pieces = length // LANES
    rows = channels * pieces
    long, twiddle, short_hi, short_lo = (jnp.asarray(t) for t in tables())
    ahead = (long, twiddle, short_hi, short_lo)
    wide = [pltpu.VMEM((2 * ROWS, 2 * LANES), bf16)] * 2
    narrow = [pltpu.VMEM((2 * ROWS, LANES), f32)]

    sources = (inputs[0], out_grad[0], next_inputs[0])
    (packed,) = call(
        pack_body, "pack", (shape((peers, 6, pieces, LANES), bf16),),
        [pltpu.VMEM((channels, length), bf16)] * 3 + [pltpu.VMEM((rows + channels, LANES), f32)] * 3
        + [pltpu.SemaphoreType.DMA((3,))],
        far=sources,
    )
    own = (2 * ROWS // owners, LANES)
    spectra = (2 * ROWS, 2 * LANES)
    partial, next_spectrum = call(
        correlate_body, "correlate", (shape((owners, *own), bf16), shape(spectra, f32)),
        [pltpu.VMEM((6 * ROWS, 2 * LANES), bf16)] * 2 + wide + narrow
        + [pltpu.VMEM(spectra, f32), pltpu.SemaphoreType.DMA((1,))],
        exchange(packed, "ctx"), *ahead, far_out=True,
    )
    new_master, new_one, new_two, filters = call(
        adam_body, "adam", (shape(own, f32),) * 3 + (shape((owners, *own), bf16),), [],
        exchange(partial, "dp"), interleave(master), interleave(moment_one), interleave(moment_two),
    )
    (result,) = call(
        convolve_body, "convolve", (shape((peers, 2, pieces, LANES), bf16),),
        wide + wide + narrow + [pltpu.VMEM(spectra, f32), pltpu.SemaphoreType.DMA((1,))],
        exchange(filters, "dp"), *ahead, far=(next_spectrum,),
    )
    (next_out,) = call(
        unpack_body, "unpack", (shape((channels, length), bf16),),
        [pltpu.VMEM((rows + channels, LANES), f32), pltpu.VMEM((channels, length), bf16)]
        + [pltpu.SemaphoreType.DMA((channels // 16,))],
        exchange(result, "ctx"), far_out=True,
    )
    return (deinterleave(new_master, 2), deinterleave(new_one, 2), deinterleave(new_two, 2), next_out[None])


def solution(mesh):
    return jax.shard_map(
        local,
        mesh=mesh,
        in_specs=(
            P("dp", None, "ctx"),
            P("dp", None, "ctx"),
            P("ctx", "dp"),
            P("ctx", "dp"),
            P("ctx", "dp"),
            P("dp", None, "ctx"),
        ),
        out_specs=(P("ctx", "dp"), P("ctx", "dp"), P("ctx", "dp"), P("dp", None, "ctx")),
        check_vma=False,
    )
```

```python
import math

import jax
import jax.numpy as jnp
import numpy as np
from jax import lax
from jax.experimental import pallas as pl
from jax.experimental.pallas import tpu as pltpu
from jax.sharding import PartitionSpec as P

ROWS = 512
LANES = 128
BLOCK = 128

f32 = jnp.float32
bf16 = jnp.bfloat16


def split_table(values):
    high = values.astype(bf16)
    low = (values - high.astype(np.float64)).astype(bf16)
    return high, low


def tables():
    half = np.arange(ROWS) + 0.5
    lanes = np.arange(LANES)
    outer = 2.0 * math.pi * np.outer(half, half) / (2 * ROWS)
    long_hi, long_lo = split_table(np.concatenate([np.cos(outer), np.sin(outer)], axis=0))
    turn = 2.0 * math.pi * np.outer(half, lanes / (2.0 * ROWS * LANES) - 1.0 / (4 * ROWS))
    twiddle = np.concatenate([np.cos(turn), np.sin(turn)], axis=1).astype(np.float32)
    inner = 2.0 * math.pi * (np.outer(lanes, lanes) % LANES) / LANES
    cosine, sine = np.cos(inner), np.sin(inner)
    short = np.block([[cosine, sine], [-sine, cosine]])
    short_hi, short_lo = split_table(short)
    fore, rear = slice(0, ROWS // 2), slice(ROWS // 2, ROWS)
    long = np.concatenate([long_hi[:, fore], long_lo[:, fore], -long_hi[:, rear], -long_lo[:, rear]], axis=1)
    return (long, twiddle, short_hi, short_lo)


def dot(left, right):
    return jnp.dot(left, right, preferred_element_type=f32)


def store_halves(values, place, high_ref, low_ref):
    high = values.astype(bf16)
    high_ref[place] = high
    low_ref[place] = (values - high.astype(f32)).astype(bf16)


def times_short(high_ref, low_ref, rows, hi_ref, lo_ref):
    left = jnp.concatenate([high_ref[rows], low_ref[rows], high_ref[rows]], axis=1)
    right = jnp.concatenate([hi_ref[...], hi_ref[...], lo_ref[...]], axis=0)
    return dot(left, right)


def channel_rows(c):
    return slice(c * ROWS, (c + 1) * ROWS)


def channel_lanes(c):
    return slice(c * LANES, (c + 1) * LANES)


LEFT, RIGHT = slice(0, LANES), slice(LANES, 2 * LANES)


def first_stage(wave, long):
    half = ROWS // 2
    fore = dot(long[:, :ROWS], jnp.concatenate([wave[:half], wave[:half]], axis=0))
    rear = dot(long[:, ROWS:], jnp.concatenate([wave[half:], wave[half:]], axis=0))
    return fore - rear


def turn(first, c, slot, twiddle, high_ref, low_ref):
    at = channel_rows(slot)
    real, imag = first[:ROWS, channel_lanes(c)], first[ROWS:, channel_lanes(c)]
    cosine, sine = twiddle[:, LEFT], twiddle[:, RIGHT]
    store_halves(real * cosine - imag * sine, (at, LEFT), high_ref, low_ref)
    store_halves(real * sine + imag * cosine, (at, RIGHT), high_ref, low_ref)


def mix(product, slot, short_hi, short_lo, high_ref, low_ref):
    store_halves(product[0], (channel_rows(slot), LEFT), high_ref, low_ref)
    store_halves(product[1], (channel_rows(slot), RIGHT), high_ref, low_ref)
    return times_short(high_ref, low_ref, channel_rows(slot), short_hi, short_lo)


def turn_back(mixed, c, twiddle, wide_hi, wide_lo):
    cosine, sine = twiddle[:, LEFT], twiddle[:, RIGHT]
    real, imag = mixed[:, LEFT], mixed[:, RIGHT]
    top, end = slice(0, ROWS), slice(ROWS, 2 * ROWS)
    store_halves(real * cosine - imag * sine, (top, channel_lanes(c)), wide_hi, wide_lo)
    store_halves(-(imag * cosine + real * sine), (end, channel_lanes(c)), wide_hi, wide_lo)


def last_stage(long, wide_hi, wide_lo):
    half = ROWS // 2
    top, end = slice(0, ROWS), slice(ROWS, 2 * ROWS)
    total = []
    for at in (0, half):
        both, high = slice(2 * at, 2 * at + ROWS), slice(2 * at, 2 * at + half)
        real, imag = slice(at, at + half), slice(ROWS + at, ROWS + at + half)
        table = jnp.concatenate([long[top, both], long[end, both], long[top, high], long[end, high]], axis=1)
        waves = [wide_hi[real], wide_hi[real], wide_hi[imag], wide_hi[imag], wide_lo[real], wide_lo[imag]]
        total.append(dot(table, jnp.concatenate(waves, axis=0)))
    return (total[0] - total[1]) * (1.0 / (ROWS * LANES))


def wave_of(ref, first):
    parts = [ref[:, first + c].reshape(ROWS, LANES) for c in range(2)]
    return jnp.concatenate(parts, axis=1)


def store_wave(ref, values):
    blocks, _, rows, _ = ref.shape
    for c in range(2):
        ref[:, c] = values[:, channel_lanes(c)].astype(bf16).reshape(blocks, rows, LANES)


def fetch(sources, places, semaphores):
    copies = [
        pltpu.make_async_copy(source, place, semaphores.at[i])
        for i, (source, place) in enumerate(zip(sources, places))
    ]
    for copy in copies:
        copy.start()
    return copies


def pack_body(*refs):
    count = (len(refs) - 2) // 3
    sources, out_ref, semaphores = refs[:count], refs[count], refs[-1]
    arrived, scratch = refs[count + 1 : 2 * count + 1], refs[2 * count + 1 : -1]
    copies = fetch(sources, arrived, semaphores)
    peers, _, pieces, _ = out_ref.shape
    for i in range(count):
        copies[i].wait()
        channels = arrived[i].shape[0]
        pitch = pieces + 1
        for k in range(pieces):
            lanes = slice(k * LANES, (k + 1) * LANES)
            scratch[i][pl.ds(k, channels, stride=pitch), :] = arrived[i][:, lanes].astype(f32)
        for c in range(channels):
            out_ref[c // 2, 2 * i + c % 2] = scratch[i][c * pitch : c * pitch + pieces, :].astype(bf16)


def unpack_body(in_ref, out_hbm, scratch, result, semaphores):
    channels, length = out_hbm.shape
    pieces = length // LANES
    pitch = pieces + 1
    group = 16
    copies = []
    for start in range(0, channels, group):
        for c in range(start, start + group):
            scratch[c * pitch : c * pitch + pieces, :] = in_ref[c // 2, c % 2].astype(f32)
        rows = pl.ds(start, group)
        for k in range(pieces):
            lanes = slice(k * LANES, (k + 1) * LANES)
            result[rows, lanes] = scratch[pl.ds(start * pitch + k, group, stride=pitch), :].astype(bf16)
        copies += fetch([result.at[rows]], [out_hbm.at[rows]], semaphores.at[pl.ds(start // group, 1)])
    for copy in copies:
        copy.wait()


def correlate_body(
    in_ref, long, twiddle, short_hi, short_lo, out_ref, next_hbm,
    high_ref, low_ref, wide_hi, wide_lo, next_spectra, semaphores,
):
    firsts = [first_stage(wave_of(in_ref, 2 * i), long) for i in range(3)]
    for c in range(2):
        spectra = []
        for w in range(2):
            turn(firsts[w], c, 3 * c + w, twiddle, high_ref, low_ref)
            spectra.append(times_short(high_ref, low_ref, channel_rows(3 * c + w), short_hi, short_lo))
        (s_re, s_im), (g_re, g_im) = [(t[:, LEFT], t[:, RIGHT]) for t in spectra]
        turn(firsts[2], c, 3 * c + 2, twiddle, high_ref, low_ref)
        next_spectra[channel_rows(c), :] = times_short(
            high_ref, low_ref, channel_rows(3 * c + 2), short_hi, short_lo
        )
        product = (g_re * s_re + g_im * s_im, g_re * s_im - g_im * s_re)
        mixed = mix(product, 3 * c, short_hi, short_lo, high_ref, low_ref)
        turn_back(mixed, c, twiddle, wide_hi, wide_lo)
    copies = fetch([next_spectra], [next_hbm], semaphores)
    result = last_stage(long, wide_hi, wide_lo)
    store_wave(out_ref, result)
    copies[0].wait()


def adam_body(grad_ref, master, one, two, new_master, new_one, new_two, filters, mixed, parted):
    total = grad_ref[0].astype(f32)
    owners, channels, rows, _ = grad_ref.shape
    for q in range(1, owners):
        total = total + grad_ref[q].astype(f32)
    for c in range(channels):
        mixed[pl.ds(c, rows, stride=channels), :] = total[c]
    grad = mixed[...]
    first = 0.9 * one[...] + 0.1 * grad
    second = 0.999 * two[...] + 0.001 * grad * grad
    first_hat = first / (1.0 - 0.9**10)
    second_hat = second / (1.0 - 0.999**10)
    old = master[...]
    new = old - 0.01 * (first_hat / (jnp.sqrt(second_hat) + 1e-08) + 0.1 * old)
    new_one[...] = first
    new_two[...] = second
    new_master[...] = new
    parted[...] = new
    for c in range(channels):
        rounded = parted[pl.ds(c, rows, stride=channels), :].astype(bf16)
        for q in range(owners):
            filters[q, c] = rounded


def convolve_body(
    in_ref, long, twiddle, short_hi, short_lo, next_hbm,
    out_ref, high_ref, low_ref, wide_hi, wide_lo, next_ref, semaphores,
):
    copies = fetch([next_hbm], [next_ref], semaphores)
    wave = wave_of(in_ref, 0)
    first = first_stage(wave, long)
    for c in range(2):
        turn(first, c, c, twiddle, high_ref, low_ref)
    copies[0].wait()
    spectra = [times_short(high_ref, low_ref, channel_rows(c), short_hi, short_lo) for c in range(2)]
    mixed = []
    for c in range(2):
        f_re, f_im = spectra[c][:, LEFT], spectra[c][:, RIGHT]
        n_re, n_im = next_ref[channel_rows(c), LEFT], next_ref[channel_rows(c), RIGHT]
        product = (f_re * n_re - f_im * n_im, -(f_re * n_im + f_im * n_re))
        mixed.append(mix(product, c, short_hi, short_lo, high_ref, low_ref))
    for c in range(2):
        turn_back(mixed[c], c, twiddle, wide_hi, wide_lo)
    result = last_stage(long, wide_hi, wide_lo)
    store_wave(out_ref, result)


def call(body, name, out_shape, scratch, *args, far=(), far_out=False, flags=None):
    near = [pltpu.with_memory_space_constraint(a, pltpu.VMEM) for a in args]
    far = [pltpu.with_memory_space_constraint(a, pltpu.HBM) for a in far]
    inside, outside = pl.BlockSpec(memory_space=pltpu.VMEM), pl.BlockSpec(memory_space=pltpu.HBM)
    out_specs = [inside] * len(out_shape)
    if far_out:
        out_specs[-1] = outside
        out_shape = (*out_shape[:-1], pltpu.HBM(out_shape[-1].shape, out_shape[-1].dtype))
    return pl.pallas_call(
        body,
        out_shape=out_shape,
        in_specs=[inside] * len(near) + [outside] * len(far),
        out_specs=tuple(out_specs),
        scratch_shapes=scratch,
        name=name,
        compiler_params=pltpu.CompilerParams(vmem_limit_bytes=16 << 20, flags=flags),
    )(*near, *far)


def shape(dims, dtype):
    return jax.ShapeDtypeStruct(dims, dtype)


def interleave(values):
    channels, taps = values.shape
    pieces = taps // LANES
    return values.reshape(channels, pieces, LANES).transpose(1, 0, 2).reshape(channels * pieces, LANES)


def deinterleave(values, channels):
    pieces = values.shape[0] // channels
    return values.reshape(pieces, channels, LANES).transpose(1, 0, 2).reshape(channels, pieces * LANES)


def exchange(values, axis):
    return lax.all_to_all(values, axis, split_axis=0, concat_axis=0, tiled=True)


def local(inputs, out_grad, master, moment_one, moment_two, next_inputs):
    channels, length = inputs.shape[1:]
    peers = lax.axis_size("ctx")
    owners = lax.axis_size("dp")
    pieces = length // LANES
    rows = channels * pieces
    long, twiddle, short_hi, short_lo = (jnp.asarray(t) for t in tables())
    ahead = (long, twiddle, short_hi, short_lo)
    wide = [pltpu.VMEM((2 * ROWS, 2 * LANES), bf16)] * 2

    sources = (inputs[0], out_grad[0], next_inputs[0])
    (packed,) = call(
        pack_body, "pack", (shape((peers, 6, pieces, LANES), bf16),),
        [pltpu.VMEM((channels, length), bf16)] * 3 + [pltpu.VMEM((rows + channels, LANES), f32)] * 3
        + [pltpu.SemaphoreType.DMA((3,))],
        far=sources,
    )
    own = (2 * ROWS // owners, LANES)
    blocks = shape((owners, 2, ROWS // owners, LANES), bf16)
    spectra = (2 * ROWS, 2 * LANES)
    partial, next_spectrum = call(
        correlate_body, "correlate", (blocks, shape(spectra, f32)),
        [pltpu.VMEM((6 * ROWS, 2 * LANES), bf16)] * 2 + wide
        + [pltpu.VMEM(spectra, f32), pltpu.SemaphoreType.DMA((1,))],
        exchange(packed, "ctx"), *ahead, far_out=True,
    )
    new_master, new_one, new_two, filters = call(
        adam_body, "adam", (shape(own, f32),) * 3 + (blocks,), [pltpu.VMEM(own, f32)] * 2,
        exchange(partial, "dp"), interleave(master), interleave(moment_one), interleave(moment_two),
    )
    (result,) = call(
        convolve_body, "convolve", (shape((peers, 2, pieces, LANES), bf16),),
        wide + wide + [pltpu.VMEM(spectra, f32), pltpu.SemaphoreType.DMA((1,))],
        exchange(filters, "dp"), *ahead, far=(next_spectrum,),
    )
    (next_out,) = call(
        unpack_body, "unpack", (shape((channels, length), bf16),),
        [pltpu.VMEM((rows + channels, LANES), f32), pltpu.VMEM((channels, length), bf16)]
        + [pltpu.SemaphoreType.DMA((channels // 16,))],
        exchange(result, "ctx"), far_out=True,
    )
    return (deinterleave(new_master, 2), deinterleave(new_one, 2), deinterleave(new_two, 2), next_out[None])


def solution(mesh):
    return jax.shard_map(
        local,
        mesh=mesh,
        in_specs=(
            P("dp", None, "ctx"),
            P("dp", None, "ctx"),
            P("ctx", "dp"),
            P("ctx", "dp"),
            P("ctx", "dp"),
            P("dp", None, "ctx"),
        ),
        out_specs=(P("ctx", "dp"), P("ctx", "dp"), P("ctx", "dp"), P("dp", None, "ctx")),
        check_vma=False,
    )
```
